32 devices in a mesh: dp: 8 (over z, y), tensor: 4 (over x, core).
Axes of the slice: x: 2, y: 2, z: 4, core: 2. Of those that a mesh axis runs over, the one named last changes fastest.
Arguments:
- inputs: bfloat16 [8192, 1536], P('dp', 'tensor'), may hold values from -6 to 6
- segment_ids: int32 [8192], P('dp'), may hold values from 0 to 26, never falling along the last dimension, each value on 1 to 1000 neighbouring positions
- cotangent: bfloat16 [8192, 1536], P('dp', 'tensor'), may hold values from -6 to 6
- first_gain: bfloat16 [1536], replicated, may hold values from 0.5 to 1.5
- gate_weight: bfloat16 [1536, 2048], P(None, 'tensor'), may hold values from -0.15625 to 0.15625
- gate_bias: bfloat16 [2048], P('tensor'), may hold values from -3 to 3
- branch_weight: bfloat16 [1536, 2048], P(None, 'tensor'), may hold values from -0.15625 to 0.15625
- branch_bias: bfloat16 [2048], P('tensor'), may hold values from -3 to 3
- conv_weight: bfloat16 [4, 2048], P(None, 'tensor'), may hold values from -3 to 3
- conv_bias: bfloat16 [2048], P('tensor'), may hold values from -3 to 3
- rate_weight: bfloat16 [16, 128, 128], P('tensor'), may hold values from -0.5 to 0.5
- rate_bias: bfloat16 [2048], P('tensor'), may hold values from -3 to 3
- input_weight: bfloat16 [16, 128, 128], P('tensor'), may hold values from -0.5 to 0.5
- input_bias: bfloat16 [2048], P('tensor'), may hold values from -3 to 3
- decay_param: float32 [2048], P('tensor'), may hold values from 3 to 7
- out_weight: bfloat16 [2048, 1536], P('tensor'), may hold values from -0.25 to 0.25
- second_gain: bfloat16 [1536], replicated, may hold values from 0.5 to 1.5
- ffn_gate: bfloat16 [1536, 4608], P(None, 'tensor'), may hold values from -0.15625 to 0.15625
- ffn_up: bfloat16 [1536, 4608], P(None, 'tensor'), may hold values from -0.15625 to 0.15625
- ffn_down: bfloat16 [4608, 1536], P('tensor'), may hold values from -0.1875 to 0.1875
Outputs:
- output: bfloat16 [8192, 1536], P('dp', 'tensor')
- input_grad: float32 [8192, 1536], P('dp', 'tensor')
- first_gain_grad: float32 [1536], replicated
- gate_weight_grad: float32 [1536, 2048], P(None, 'tensor')
- gate_bias_grad: float32 [2048], P('tensor')
- branch_weight_grad: float32 [1536, 2048], P(None, 'tensor')
- branch_bias_grad: float32 [2048], P('tensor')
- conv_weight_grad: float32 [4, 2048], P(None, 'tensor')
- conv_bias_grad: float32 [2048], P('tensor')
- rate_weight_grad: float32 [16, 128, 128], P('tensor')
- rate_bias_grad: float32 [2048], P('tensor')
- input_weight_grad: float32 [16, 128, 128], P('tensor')
- input_bias_grad: float32 [2048], P('tensor')
- decay_grad: float32 [2048], P('tensor')
- out_weight_grad: float32 [2048, 1536], P('tensor')
- second_gain_grad: float32 [1536], replicated
- ffn_gate_grad: float32 [1536, 4608], P(None, 'tensor')
- ffn_up_grad: float32 [1536, 4608], P(None, 'tensor')
- ffn_down_grad: float32 [4608, 1536], P('tensor')
The draws below stay inside these ranges and needn't reach their ends.
Inputs may be any that keep to these rules, and one draw needn't show every extreme that they name: `segment_ids`: segment numbers never fall along the tokens; each document has 1 to 1000 consecutive tokens, one exactly 1000.
All inputs are finite; a program needn't handle non-finite values.
Results may differ from the reference program's by a relative error of at most 0.013.
Values may be sent and summed in bfloat16 or wider, within the bound.
A program may use at most 256 MiB of HBM per device.

```python
import math
import jax
import jax.numpy as jnp
import numpy as np
from jax import lax

D = 1536
R = 2048
H = 16
FF = 4608
BW = 128
CONV = 4
SEQ = 1024
TOK_DEV = 1024
TOKENS = 8192
SEG_COUNT = 27
DOC_MOST = 1000
N_DP = 8


def block_levels(own_key, extent, cuts, low, high):
    factor_of = 1.0
    for axis_at, shards_of in cuts:
        draws = jax.random.uniform(jax.random.fold_in(jax.random.fold_in(own_key, 6), axis_at), (shards_of,), jnp.float32, low / len(cuts), high / len(cuts))
        factor_of = factor_of * jnp.repeat(jnp.exp(draws), extent[axis_at] // shards_of).reshape((-1,) + (1,) * (len(extent) - 1 - axis_at))
    return factor_of


def split_up(count, total, most, slope):
    loads = [(1 << 20) // math.isqrt(standing ** slope) + 1 for standing in range(2, count + 1)]
    rest, given = total - most - (count - 1), [1] * (count - 1)
    while rest > 0:
        free = [i for i in range(count - 1) if given[i] < most]
        whole, remaining = sum([loads[i] for i in free]), rest
        for i in free:
            extra = min(most - given[i], max(1, remaining * loads[i] // whole), rest)
            given[i] = given[i] + extra
            rest = rest - extra
    return np.array([most] + given)


def uneven(own_key, amount, total, bound, slope):
    if amount == 2:
        one = jax.random.randint(own_key, (), max(1, total - bound), min(bound, total - 1) + 1)
        return jnp.stack([one, total - one])
    tallies = jnp.asarray(split_up(amount, total, bound, slope), jnp.int32)
    twos = (amount - 1) // 2
    source_of, taker = tallies[1:1 + 2 * twos:2], tallies[2:2 + 2 * twos:2]
    slack = jnp.minimum(source_of - 1, bound - taker)
    shifted = jax.random.randint(jax.random.fold_in(own_key, 1), (twos,), 0, 1 << 20) % (slack + 1)
    tallies = tallies.at[1:1 + 2 * twos:2].set(source_of - shifted).at[2:2 + 2 * twos:2].set(taker + shifted)
    return tallies[jax.random.permutation(jax.random.fold_in(own_key, 2), amount)]


def scatter_about(rng, shape, spread, bound, pieces=(), kind=jnp.bfloat16):
    factor_of = block_levels(rng, shape, pieces, -0.22, 0.18) if pieces else 1.0
    entries = jax.random.normal(rng, shape, jnp.float32) * spread * factor_of
    return jnp.minimum(jnp.maximum(entries, -bound), bound).astype(kind)


def setup_inputs(seed: int = 0) -> dict:
    arg_keys = jax.random.split(jax.random.key(seed), 21)
    return {
        "inputs": scatter_about(arg_keys[0], (TOKENS, D), 1.0, 6.0, ((0, 8), (1, 4))),
        "segment_ids": jnp.searchsorted(jnp.cumsum(uneven(arg_keys[1], SEG_COUNT, TOKENS, DOC_MOST, 0)), jnp.arange(TOKENS), side="right").astype(jnp.int32),
        "cotangent": scatter_about(arg_keys[2], (TOKENS, D), 1.0, 6.0, ((0, 8), (1, 4))),
        "first_gain": jnp.clip(1.0 + 0.1 * jax.random.normal(arg_keys[3], (D,), jnp.float32), 0.5, 1.5).astype(jnp.bfloat16),
        "gate_weight": scatter_about(arg_keys[4], (D, R), D ** -0.5, 0.15625, ((1, 4),)),
        "gate_bias": scatter_about(arg_keys[5], (R,), 0.5, 3.0, ((0, 4),)),
        "branch_weight": scatter_about(arg_keys[6], (D, R), D ** -0.5, 0.15625, ((1, 4),)),
        "branch_bias": scatter_about(arg_keys[7], (R,), 0.5, 3.0, ((0, 4),)),
        "conv_weight": scatter_about(arg_keys[8], (CONV, R), CONV ** -0.5, 3.0, ((1, 4),)),
        "conv_bias": scatter_about(arg_keys[9], (R,), 0.5, 3.0, ((0, 4),)),
        "rate_weight": scatter_about(arg_keys[10], (H, BW, BW), BW ** -0.5, 0.5, ((0, 4),)),
        "rate_bias": scatter_about(arg_keys[11], (R,), 0.5, 3.0, ((0, 4),)),
        "input_weight": scatter_about(arg_keys[12], (H, BW, BW), BW ** -0.5, 0.5, ((0, 4),)),
        "input_bias": scatter_about(arg_keys[13], (R,), 0.5, 3.0, ((0, 4),)),
        "decay_param": jnp.clip(3.0 + 4.0 * jax.random.uniform(arg_keys[14], (R,), jnp.float32) ** block_levels(arg_keys[14], (R,), ((0, 4),), -0.2, 0.2), 3.0, 7.0),
        "out_weight": scatter_about(arg_keys[15], (R, D), (R // 4) ** -0.5, 0.25, ((0, 4),)),
        "second_gain": jnp.clip(1.0 + 0.1 * jax.random.normal(arg_keys[16], (D,), jnp.float32), 0.5, 1.5).astype(jnp.bfloat16),
        "ffn_gate": scatter_about(arg_keys[17], (D, FF), D ** -0.5, 0.15625, ((1, 4),)),
        "ffn_up": scatter_about(arg_keys[18], (D, FF), D ** -0.5, 0.15625, ((1, 4),)),
        "ffn_down": scatter_about(arg_keys[19], (FF, D), (FF // 4) ** -0.5, 0.1875, ((0, 4),)),
    }


@jax.custom_vjp
def low(v):
    return lax.optimization_barrier(v.astype(jnp.bfloat16)).astype(jnp.float32)

@jax.custom_vjp
def low_back(v):
    return v

def low_keep(v):
    return (low(v), None)

def low_pass(kept, grad):
    return (grad,)

def back_keep(v):
    return (v, None)

def back_low(kept, grad):
    return (low(grad),)
low.defvjp(low_keep, low_pass)
low_back.defvjp(back_keep, back_low)
EPSILON = 1e-06
FLOOR = 0.05

def product(left, right):
    return jnp.dot(left, right, precision=lax.Precision.HIGHEST)

def rms_scale(values, gain):
    return values * lax.rsqrt(lax.optimization_barrier(jnp.mean(values * values, axis=-1, keepdims=True)) + EPSILON) * gain

def seq_masks(segments, length):
    count = segments.shape[0]
    place = jnp.arange(count, dtype=jnp.int32) % length
    previous = jnp.concatenate([segments[:1], segments[:-1]])
    reset = (place == 0) | (segments != previous)
    return (place, reset)

def conv_apply(values, weights, shift_bias, segments, place):
    total = shift_bias + weights[0] * values
    for offset in range(1, weights.shape[0]):
        moved = jnp.concatenate([jnp.zeros((offset, values.shape[1]), values.dtype), values[:-offset]])
        earlier = jnp.concatenate([jnp.full((offset,), -1, jnp.int32), segments[:-offset]])
        usable = ((place >= offset) & (segments == earlier)).astype(values.dtype)
        total = total + weights[offset] * moved * usable[:, None]
    return total

def block_mix(values, weight):
    rows = values.shape[0]
    split = values.reshape(rows, weight.shape[0], -1)
    return jnp.einsum('thi,hij->thj', split, weight, precision=lax.Precision.HIGHEST).reshape(rows, -1)

def gates_to_step(rate_pre, input_pre, conv_out, decay, reset):
    rate = jax.nn.sigmoid(rate_pre)
    opened = jax.nn.sigmoid(input_pre)
    decayed = jnp.exp(-8.0 * rate * jax.nn.softplus(-decay))
    keep = jnp.where(reset[:, None], jnp.zeros_like(decayed), decayed)
    scale = jnp.where(reset[:, None], jnp.ones_like(decayed), jnp.sqrt(jnp.maximum(1.0 - decayed * decayed, FLOOR)))
    return (keep, scale * opened * conv_out)

def combine(earlier, later):
    return (earlier[0] * later[0], later[0] * earlier[1] + later[1])

def block_forward(weights, inputs_f, segments):
    first_gain, gate_weight, gate_bias, branch_weight, branch_bias, conv_weight, conv_bias, rate_weight, rate_bias, input_weight, input_bias, decay_param, out_weight, second_gain, ffn_gate, ffn_up, ffn_down = weights
    place, reset = seq_masks(segments, SEQ)
    normed_one = low(rms_scale(inputs_f, first_gain))
    gate_pre = low_back(product(normed_one, gate_weight) + gate_bias)
    branch_pre = low_back(product(normed_one, branch_weight) + branch_bias)
    conv_out = conv_apply(branch_pre, conv_weight, conv_bias, segments, place)
    conv_low = low(conv_out)
    rate_pre = low_back(block_mix(conv_low, rate_weight) + rate_bias)
    input_pre = low_back(block_mix(conv_low, input_weight) + input_bias)
    keep, drive = gates_to_step(rate_pre, input_pre, conv_out, decay_param, reset)
    state = lax.associative_scan(combine, (keep, drive))[1]
    mixed = low(jax.nn.gelu(gate_pre) * state)
    resid = inputs_f + low_back(product(mixed, out_weight))
    normed_two = low(rms_scale(resid, second_gain))
    hidden_gate = low_back(product(normed_two, ffn_gate))
    hidden_up = low_back(product(normed_two, ffn_up))
    hidden = low(jax.nn.gelu(hidden_gate) * hidden_up)
    return resid + low_back(product(hidden, ffn_down))

def reference(inputs, segment_ids, cotangent, first_gain, gate_weight, gate_bias, branch_weight, branch_bias, conv_weight, conv_bias, rate_weight, rate_bias, input_weight, input_bias, decay_param, out_weight, second_gain, ffn_gate, ffn_up, ffn_down):
    weights = tuple((item.astype(jnp.float32) for item in (first_gain, gate_weight, gate_bias, branch_weight, branch_bias, conv_weight, conv_bias, rate_weight, rate_bias, input_weight, input_bias, decay_param, out_weight, second_gain, ffn_gate, ffn_up, ffn_down)))
    grouped_in = inputs.astype(jnp.float32).reshape(N_DP, TOK_DEV, D)
    grouped_seg = segment_ids.reshape(N_DP, TOK_DEV)
    grouped_cot = cotangent.astype(jnp.float32).reshape(N_DP, TOK_DEV, D)

    def one_group(totals, item):
        group_in, group_seg, group_cot = item

        def forward(params, values):
            return block_forward(params, values, group_seg)
        result, pull = jax.vjp(forward, weights, group_in)
        grads, in_grad = pull(group_cot)
        return (tuple((left + right for left, right in zip(totals, grads))), (result.astype(jnp.bfloat16), in_grad))
    starting = tuple((jnp.zeros_like(item) for item in weights))
    totals, (outs, in_grads) = lax.scan(one_group, starting, (grouped_in, grouped_seg, grouped_cot))
    return (outs.reshape(TOKENS, D), in_grads.reshape(TOKENS, D), totals[0], totals[1], totals[2], totals[3], totals[4], totals[5], totals[6], totals[7], totals[8], totals[9], totals[10], totals[11], totals[12], totals[13], totals[14], totals[15], totals[16])
```

```python
import functools

import jax
import jax.numpy as jnp
from jax import lax
from jax.experimental import pallas as pl
from jax.experimental.pallas import tpu as pltpu
from jax.sharding import PartitionSpec as P

EPSILON = 1e-06
FLOOR = 0.05
F32 = jnp.float32
BF16 = jnp.bfloat16
LANES = 128
SPAN = 32
HALO = 8
MIB = 1024 * 1024


def params(mib, **more):
    return pltpu.CompilerParams(vmem_limit_bytes=mib * MIB, **more)


def gelu_parts(v):
    c0 = 0.7978845608028654
    c1 = 0.044715
    t = jnp.tanh(c0 * (v + c1 * v * v * v))
    act = 0.5 * v * (1.0 + t)
    slope = 0.5 * (1.0 + t) + 0.5 * v * (1.0 - t * t) * c0 * (1.0 + 3.0 * c1 * v * v)
    return act, slope


def sigmoid(v):
    return 0.5 * jnp.tanh(0.5 * v) + 0.5


def shift_down(v, amount, fill):
    row = lax.broadcasted_iota(jnp.int32, v.shape, 0)
    return jnp.where(row >= amount, pltpu.roll(v, amount, 0), fill)


def shift_up(v, amount, fill):
    row = lax.broadcasted_iota(jnp.int32, v.shape, 0)
    size = v.shape[0]
    return jnp.where(row < size - amount, pltpu.roll(v, size - amount, 0), fill)


def scale_of(decayed, reset):
    rest = 1.0 - decayed * decayed
    return jnp.where(reset, 1.0, jnp.sqrt(jnp.maximum(rest, FLOOR))), rest


def forward_kernel(
    gate_ref, branch_ref, mask_ref, row_ref, rate_w, input_w,
    conv_out, rate_out, open_out, state_out, mixed_out, padded, keep_s, local_s,
):
    tokens = gate_ref.shape[0]
    step = 128
    spans = tokens // SPAN
    padded[0:HALO, :] = jnp.zeros((HALO, LANES), F32)
    padded[HALO:, :] = branch_ref[...]
    wr = rate_w[0]
    wi = input_w[0]

    def fill(i, carry):
        r0 = pl.multiple_of(i * step, step)
        here = pl.ds(r0, step)
        wide = padded[pl.ds(r0, step + HALO), :]
        total = row_ref[4:5, :] + row_ref[0:1, :] * wide[HALO:, :]
        for k in range(1, 4):
            total = total + row_ref[k : k + 1, :] * wide[HALO - k : HALO - k + step, :] * mask_ref[here, k : k + 1]
        low = total.astype(BF16)
        rate = sigmoid(jnp.dot(low, wr, preferred_element_type=F32) + row_ref[5:6, :])
        opened = sigmoid(jnp.dot(low, wi, preferred_element_type=F32) + row_ref[6:7, :])
        reset = mask_ref[here, 0:1] > 0.5
        decayed = jnp.exp(-8.0 * rate * row_ref[7:8, :])
        scale, _ = scale_of(decayed, reset)
        conv_out[here, :] = total
        rate_out[here, :] = rate
        open_out[here, :] = opened
        keep_s[here, :] = jnp.where(reset, 0.0, decayed)
        state_out[here, :] = scale * opened * total
        return carry

    lax.fori_loop(0, tokens // step, fill, 0)
    h = jnp.zeros((spans, LANES), F32)
    p = jnp.ones((spans, LANES), F32)
    for k in range(SPAN):
        at = pl.ds(k, spans, stride=SPAN)
        a = keep_s[at, :]
        h = a * h + state_out[at, :]
        p = p * a
        local_s[at, :] = h
        keep_s[at, :] = p
    jump = 1
    while jump < spans:
        h = h + p * shift_down(h, jump, 0.0)
        p = p * shift_down(p, jump, 1.0)
        jump *= 2
    carry_in = shift_down(h, 1, 0.0)
    for k in range(SPAN):
        at = pl.ds(k, spans, stride=SPAN)
        state_out[at, :] = local_s[at, :] + keep_s[at, :] * carry_in

    def mix(i, carry):
        here = pl.ds(pl.multiple_of(i * step, step), step)
        act, _ = gelu_parts(gate_ref[here, :])
        mixed_out[here, :] = (act * state_out[here, :]).astype(BF16)
        return carry

    lax.fori_loop(0, tokens // step, mix, 0)


def forward_block(gate_pre, branch_pre, masks, rows, rate_weight, input_weight):
    tokens, channels = gate_pre.shape
    heads = rate_weight.shape[0]
    col = pl.BlockSpec((tokens, LANES), lambda h: (0, h))
    whole = pl.BlockSpec(masks.shape, lambda h: (0, 0))
    table = pl.BlockSpec((8, LANES), lambda h: (0, h))
    square = pl.BlockSpec((1, LANES, LANES), lambda h: (h, 0, 0))
    full = jax.ShapeDtypeStruct((tokens, channels), F32)
    return pl.pallas_call(
        forward_kernel,
        grid=(heads,),
        in_specs=[col, col, whole, table, square, square],
        out_specs=[col] * 5,
        out_shape=[full] * 4 + [jax.ShapeDtypeStruct((tokens, channels), BF16)],
        scratch_shapes=[
            pltpu.VMEM((tokens + HALO, LANES), F32),
            pltpu.VMEM((tokens, LANES), F32),
            pltpu.VMEM((tokens, LANES), F32),
        ],
        compiler_params=params(24),
        cost_estimate=pl.CostEstimate(flops=tokens * channels * 700, bytes_accessed=tokens * channels * 26, transcendentals=tokens * channels * 5),
        name="recurrence_forward",
    )(gate_pre, branch_pre, masks, rows, rate_weight, input_weight)


def column_total(v):
    return jnp.sum(v, axis=0, keepdims=True)


def backward_kernel(
    dmix_ref, gate_ref, branch_ref, conv_ref, rate_ref, open_ref, state_ref, mask_ref, row_ref, rate_w, input_w,
    dgate_out, dbranch_out, misc_out, padded, keep_s, adj_s, dconv_s, prev_s, rate_g, input_g, small_g,
):
    tokens = gate_ref.shape[0]
    step = 128
    count = tokens // step
    spans = tokens // SPAN
    zero_halo = jnp.zeros((HALO, LANES), F32)
    padded[0:HALO, :] = zero_halo
    padded[HALO:, :] = branch_ref[...]
    prev_s[0:HALO, :] = zero_halo
    prev_s[HALO:, :] = state_ref[...]
    keep_s[tokens:, :] = zero_halo
    dconv_s[tokens:, :] = zero_halo
    wr = rate_w[0]
    wi = input_w[0]

    def fill(i, total):
        here = pl.ds(pl.multiple_of(i * step, step), step)
        act, slope = gelu_parts(gate_ref[here, :])
        dmix = dmix_ref[here, :]
        dgate = (dmix * state_ref[here, :] * slope).astype(BF16)
        dgate_out[here, :] = dgate
        adj_s[here, :] = dmix * act
        reset = mask_ref[here, 0:1] > 0.5
        keep_s[here, :] = jnp.where(reset, 0.0, jnp.exp(-8.0 * rate_ref[here, :] * row_ref[7:8, :]))
        return total + column_total(dgate.astype(F32))

    gate_bias = lax.fori_loop(0, count, fill, jnp.zeros((1, LANES), F32))
    h = jnp.zeros((spans, LANES), F32)
    p = jnp.ones((spans, LANES), F32)
    for k in reversed(range(SPAN)):
        at = pl.ds(k, spans, stride=SPAN)
        a = keep_s[pl.ds(k + 1, spans, stride=SPAN), :]
        h = a * h + adj_s[at, :]
        p = p * a
        adj_s[at, :] = h
        dconv_s[at, :] = p
    jump = 1
    while jump < spans:
        h = h + p * shift_up(h, jump, 0.0)
        p = p * shift_up(p, jump, 1.0)
        jump *= 2
    carry_in = shift_up(h, 1, 0.0)
    for k in range(SPAN):
        at = pl.ds(k, spans, stride=SPAN)
        adj_s[at, :] = adj_s[at, :] + dconv_s[at, :] * carry_in

    nothing = jnp.zeros((1, LANES), F32)
    rate_g[...] = jnp.zeros_like(rate_g)
    input_g[...] = jnp.zeros_like(input_g)

    def gates(i, totals):
        r0 = pl.multiple_of(i * step, step)
        here = pl.ds(r0, step)
        adj = adj_s[here, :]
        conv = conv_ref[here, :]
        rate = rate_ref[here, :]
        opened = open_ref[here, :]
        reset = mask_ref[here, 0:1] > 0.5
        decay_row = row_ref[7:8, :]
        decayed = jnp.exp(-8.0 * rate * decay_row)
        scale, rest = scale_of(decayed, reset)
        before = prev_s[pl.ds(r0, step + HALO), :][HALO - 1 : HALO - 1 + step, :]
        pull = jnp.where(rest > FLOOR, 1.0, jnp.where(rest == FLOOR, 0.5, 0.0))
        d_scale = adj * opened * conv
        d_decayed = jnp.where(reset, 0.0, adj * before - d_scale * pull * decayed / scale)
        d_log = d_decayed * decayed * -8.0
        d_rate = (d_log * decay_row * rate * (1.0 - rate)).astype(BF16)
        d_input = (adj * scale * conv * opened * (1.0 - opened)).astype(BF16)
        d_conv = (
            adj * scale * opened
            + lax.dot_general(d_rate, wr, (((1,), (1,)), ((), ())), preferred_element_type=F32)
            + lax.dot_general(d_input, wi, (((1,), (1,)), ((), ())), preferred_element_type=F32)
        )
        dconv_s[here, :] = d_conv
        low = conv.astype(BF16)
        rate_g[...] += lax.dot_general(low, d_rate, (((0,), (0,)), ((), ())), preferred_element_type=F32)
        input_g[...] += lax.dot_general(low, d_input, (((0,), (0,)), ((), ())), preferred_element_type=F32)
        wide = padded[pl.ds(r0, step + HALO), :]
        news = [
            column_total(d_conv * wide[HALO:, :]),
            *[
                column_total(d_conv * mask_ref[here, k : k + 1] * wide[HALO - k : HALO - k + step, :])
                for k in range(1, 4)
            ],
            column_total(d_conv),
            column_total(d_rate.astype(F32)),
            column_total(d_input.astype(F32)),
            column_total(d_log * rate),
        ]
        return tuple(t + n for t, n in zip(totals, news))

    totals = lax.fori_loop(0, count, gates, (nothing,) * 8)

    def conv_back(i, total):
        r0 = pl.multiple_of(i * step, step)
        here = pl.ds(r0, step)
        wide = dconv_s[pl.ds(r0, step + HALO), :]
        d_branch = row_ref[0:1, :] * wide[:step, :]
        for k in range(1, 4):
            part = wide * mask_ref[pl.ds(r0, step + HALO), k : k + 1]
            d_branch = d_branch + row_ref[k : k + 1, :] * part[k : k + step, :]
        low = d_branch.astype(BF16)
        dbranch_out[here, :] = low
        return total + column_total(low.astype(F32))

    branch_bias = lax.fori_loop(0, count, conv_back, nothing)
    small_g[...] = jnp.zeros_like(small_g)
    for at, value in enumerate((*totals, gate_bias, branch_bias)):
        small_g[at : at + 1, :] = value
    misc_out[...] = jnp.zeros_like(misc_out)
    misc_out[0:LANES, :] = rate_g[...].astype(BF16)
    misc_out[LANES : 2 * LANES, :] = input_g[...].astype(BF16)
    misc_out[2 * LANES : 2 * LANES + 16, :] = small_g[...].astype(BF16)


def backward_block(d_mixed, gate_pre, branch_pre, conv, rate, opened, state, masks, rows, rate_weight, input_weight):
    tokens, channels = gate_pre.shape
    heads = rate_weight.shape[0]
    col = pl.BlockSpec((tokens, LANES), lambda h: (0, h))
    whole = pl.BlockSpec(masks.shape, lambda h: (0, 0))
    table = pl.BlockSpec((8, LANES), lambda h: (0, h))
    square = pl.BlockSpec((1, LANES, LANES), lambda h: (h, 0, 0))
    misc = pl.BlockSpec((3 * LANES, LANES), lambda h: (0, h))
    return pl.pallas_call(
        backward_kernel,
        grid=(heads,),
        in_specs=[col] * 7 + [whole, table, square, square],
        out_specs=[col, col, misc],
        out_shape=[
            jax.ShapeDtypeStruct((tokens, channels), BF16),
            jax.ShapeDtypeStruct((tokens, channels), BF16),
            jax.ShapeDtypeStruct((3 * LANES, channels), BF16),
        ],
        scratch_shapes=[
            pltpu.VMEM((tokens + HALO, LANES), F32),
            pltpu.VMEM((tokens + HALO, LANES), F32),
            pltpu.VMEM((tokens, LANES), F32),
            pltpu.VMEM((tokens + HALO, LANES), F32),
            pltpu.VMEM((tokens + HALO, LANES), F32),
            pltpu.VMEM((LANES, LANES), F32),
            pltpu.VMEM((LANES, LANES), F32),
            pltpu.VMEM((16, LANES), F32),
        ],
        compiler_params=params(24),
        cost_estimate=pl.CostEstimate(flops=tokens * channels * 1400, bytes_accessed=tokens * channels * 32, transcendentals=tokens * channels * 5),
        name="recurrence_backward",
    )(d_mixed, gate_pre, branch_pre, conv, rate, opened, state, masks, rows, rate_weight, input_weight)


X_PAIRS = [(0, 2), (2, 0), (1, 3), (3, 1)]
CORE_PAIRS = [(0, 1), (1, 0), (2, 3), (3, 2)]


def swap_x(v):
    return lax.ppermute(v, "tensor", X_PAIRS)


def swap_core(v):
    return lax.ppermute(v, "tensor", CORE_PAIRS)


def place():
    at = lax.axis_index("tensor")
    return at // 2, at % 2


def share_features(v):
    across = swap_x(v)
    return v, swap_core(v), across, swap_core(across)


def join_features(pieces):
    at = lax.axis_index("tensor")
    rows, share = pieces[0].shape
    out = jnp.zeros((rows, share * 4), pieces[0].dtype)
    for distance, piece in enumerate(pieces):
        out = lax.dynamic_update_slice_in_dim(out, piece, (at ^ distance) * share, 1)
    return out


def token_start(tokens):
    x, core = place()
    return (core * 2 + x) * (tokens // 4)


def scatter_tokens(v):
    x, core = place()
    half = v.shape[0] // 2
    mine = lax.dynamic_slice_in_dim(v, core * half, half, 0)
    other = lax.dynamic_slice_in_dim(v, (1 - core) * half, half, 0)
    both = mine + swap_core(other.astype(BF16)).astype(F32)
    quarter = half // 2
    mine = lax.dynamic_slice_in_dim(both, x * quarter, quarter, 0)
    other = lax.dynamic_slice_in_dim(both, (1 - x) * quarter, quarter, 0)
    return mine + swap_x(other.astype(BF16)).astype(F32)


def gather_tokens(v):
    x, core = place()
    block = v.shape[0]
    across = swap_x(v)
    near = swap_core(v)
    far = swap_core(across)
    out = jnp.zeros((block * 4, v.shape[1]), v.dtype)
    for piece, where in (
        (v, core * 2 + x),
        (near, (1 - core) * 2 + x),
        (across, core * 2 + 1 - x),
        (far, (1 - core) * 2 + 1 - x),
    ):
        out = lax.dynamic_update_slice_in_dim(out, piece, where * block, 0)
    return out


def scatter_features(v):
    x, core = place()
    share = v.shape[1] // 4

    def part(at):
        return lax.dynamic_slice_in_dim(v, at * share, share, 1)

    def pair(c):
        return part(x * 2 + c), part((1 - x) * 2 + c)

    mine, other = pair(core)
    send_mine, send_other = pair(1 - core)
    got_mine = swap_core(send_mine.astype(BF16)).astype(F32)
    got_other = swap_core(send_other.astype(BF16)).astype(F32)
    return mine + got_mine, swap_x((other + got_other).astype(BF16))


def tensor_sum(v):
    v = v + swap_core(v)
    return v + swap_x(v)


MESH = pl.DeviceIdType.MESH


def ring_kernel(count, n, *refs):
    ins, extra, refs = refs[:count], refs[count : count + 4], refs[count + 4 :]
    outs, sums, refs = refs[:count], refs[count : count + 2], refs[count + 2 :]
    slots, locals_, refs = refs[:count], refs[count : 2 * count], refs[2 * count :]
    send_sem, recv_sem, load_sem, keep_sem = refs[:4]
    held, core_send, core_recv, x_send, x_recv, own, other, held_sem, share_send, share_recv = (
        refs[4:8], *refs[8:]
    )
    hidden_s, down_s, resid_s, first_s = held
    me = lax.axis_index("dp")
    y = lax.rem(me, 2)
    z = me // 2
    p = jnp.where(y == 0, z, n - 1 - z)

    def device(at):
        return jnp.where(at < n // 2, 2 * at, 2 * (n - 1 - at) + 1)

    after, before = device(lax.rem(p + 1, n)), device(lax.rem(p + n - 1, n))
    targets = (after, before)
    at = lax.axis_index("tensor")
    core = lax.rem(at, 2)
    x = at // 2
    core_peer = x * 2 + 1 - core
    x_peer = (1 - x) * 2 + core
    barrier = pltpu.get_barrier_semaphore()
    for target in targets:
        pl.semaphore_signal(barrier, inc=1, device_id={"dp": target}, device_id_type=MESH)
    for target in (core_peer, x_peer):
        pl.semaphore_signal(barrier, inc=1, device_id={"tensor": target}, device_id_type=MESH)
    pl.semaphore_wait(barrier, 4)

    def hold(i):
        return pltpu.make_async_copy(extra[i], held[i], held_sem.at[i])

    for i in range(4):
        hold(i).start()
    tokens, share = own.shape[1:]
    block = tokens // 4

    def share_copy(kind, i):
        if i < 2:
            source, target, device = core_send.at[kind, i], core_recv.at[kind, i], core_peer
        else:
            source, target, device = x_send.at[kind], x_recv.at[kind], x_peer
        return pltpu.make_async_remote_copy(
            source, target, share_send.at[kind, i], share_recv.at[kind, i],
            device_id={"tensor": device}, device_id_type=MESH,
        )

    def output_term(b, rows, cols):
        mine = jnp.where(b == core * 2 + x, 1.0, 0.0)
        return jnp.dot(hidden_s[rows, :], down_s[:, cols], preferred_element_type=F32) + mine * resid_s[:, cols]

    def first_term(b, rows, cols):
        return first_s[rows, cols]

    def share_terms(kind, term):
        def run(b, carry):
            rows = pl.ds(pl.multiple_of(b * block, block), block)
            for xx, c, ref in (
                (1 - x, 1 - core, core_send.at[kind, 1]),
                (x, 1 - core, core_send.at[kind, 0]),
                (1 - x, core, other.at[kind]),
                (x, core, own.at[kind]),
            ):
                cols = pl.ds(pl.multiple_of((xx * 2 + c) * share, LANES), share)
                ref[rows, :] = term(b, rows, cols).astype(ref.dtype)
            return carry

        lax.fori_loop(0, 4, run, 0)
        share_copy(kind, 1).start()
        share_copy(kind, 0).start()

    def share_forward(kind):
        share_copy(kind, 1).wait_recv()
        x_send[kind] = (other[kind] + core_recv[kind, 1].astype(F32)).astype(BF16)
        share_copy(kind, 2).start()

    def share_finish(kind):
        share_copy(kind, 0).wait_recv()
        share_copy(kind, 2).wait_recv()
        total = own[kind] + core_recv[kind, 0].astype(F32) + x_recv[kind].astype(F32)
        sums[kind][...] = total.astype(sums[kind].dtype)

    def piece(ref, q, side, chunk):
        rows = ref.shape[0] // (2 * n)
        start = pl.multiple_of((2 * lax.rem(chunk + n, n) + side) * rows, 8)
        return ref.at[pl.ds(start, rows), :]

    def arriving(side, s):
        if s < n - 1:
            return p - 1 - s if side == 0 else p + 1 + s
        s -= n - 1
        return p - s if side == 0 else p + s

    def send(q, side, s, source):
        if s < n - 1:
            target = slots[q].at[s, side]
        else:
            chunk = p + 1 - (s - n + 1) if side == 0 else p - 1 + (s - n + 1)
            target = piece(outs[q], q, side, chunk + n)
        copy = pltpu.make_async_remote_copy(
            source, target, send_sem.at[q, side, s], recv_sem.at[q, side, s],
            device_id={"dp": targets[side]}, device_id_type=MESH,
        )
        copy.start()

    def wait(q, side, s, which):
        if s < n - 1:
            shape = slots[q].at[s, side]
        else:
            shape = piece(outs[q], q, side, arriving(side, s) + n)
        copy = pltpu.make_async_remote_copy(
            shape, shape, send_sem.at[q, side, s], recv_sem.at[q, side, s],
            device_id={"dp": targets[side]}, device_id_type=MESH,
        )
        (copy.wait_recv if which else copy.wait_send)()

    def load(q, side, s):
        return pltpu.make_async_copy(
            piece(ins[q], q, side, arriving(side, s) + n), locals_[q].at[s % 2, side], load_sem.at[q, side, s % 2]
        )

    for q in range(count):
        for side in range(2):
            send(q, side, 0, piece(ins[q], q, side, p + n))
    for q in range(count):
        for side in range(2):
            load(q, side, 0).start()
    for i in range(4):
        hold(i).wait()
    share_terms(0, output_term)
    share_terms(1, first_term)
    for s in range(n - 1):
        if s == 1:
            share_forward(0)
            share_forward(1)
        if s == 4:
            share_finish(0)
            share_finish(1)
        for q in range(count):
            for side in range(2):
                if s + 1 < n - 1:
                    load(q, side, s + 1).start()
                load(q, side, s).wait()
                wait(q, side, s, True)
                slot = slots[q].at[s, side]
                slot[...] = (slot[...].astype(F32) + locals_[q][s % 2, side].astype(F32)).astype(BF16)
                send(q, side, s + 1, slot)
                if s == n - 2:
                    chunk = p + 1 if side == 0 else p - 1
                    pltpu.make_async_copy(slot, piece(outs[q], q, side, chunk + n), keep_sem.at[q, side]).start()
    for s in range(n - 1, 2 * n - 2):
        for q in range(count):
            for side in range(2):
                wait(q, side, s, True)
                if s + 1 < 2 * n - 2:
                    send(q, side, s + 1, piece(outs[q], q, side, arriving(side, s) + n))
    for q in range(count):
        for side in range(2):
            slot = slots[q].at[n - 2, side]
            chunk = p + 1 if side == 0 else p - 1
            pltpu.make_async_copy(slot, piece(outs[q], q, side, chunk + n), keep_sem.at[q, side]).wait()
            for s in range(2 * n - 2):
                wait(q, side, s, False)
    for kind in range(2):
        for i in range(3):
            share_copy(kind, i).wait_send()


def ring_all(arrays, hidden, down, resid, first):
    n = 8
    count = len(arrays)
    halves = [(a.shape[0] // (2 * n), a.shape[1]) for a in arrays]
    size = sum(a.size for a in arrays)
    extra = (hidden, down, resid, first)
    tokens = hidden.shape[0]
    share = down.shape[1] // 4
    hbm = pl.BlockSpec(memory_space=pl.ANY)
    out = pl.pallas_call(
        functools.partial(ring_kernel, count, n),
        in_specs=[hbm] * (count + 4),
        out_specs=[hbm] * count + [pl.BlockSpec(memory_space=pltpu.VMEM)] * 2,
        out_shape=[
            *[jax.ShapeDtypeStruct(a.shape, BF16) for a in arrays],
            jax.ShapeDtypeStruct((tokens, share), BF16),
            jax.ShapeDtypeStruct((tokens, share), F32),
        ],
        scratch_shapes=[
            *[pltpu.VMEM((n - 1, 2, *h), BF16) for h in halves],
            *[pltpu.VMEM((2, 2, *h), BF16) for h in halves],
            pltpu.SemaphoreType.DMA((count, 2, 2 * n - 2)),
            pltpu.SemaphoreType.DMA((count, 2, 2 * n - 2)),
            pltpu.SemaphoreType.DMA((count, 2, 2)),
            pltpu.SemaphoreType.DMA((count, 2)),
            *[pltpu.VMEM(a.shape, a.dtype) for a in extra],
            pltpu.VMEM((2, 2, tokens, share), BF16),
            pltpu.VMEM((2, 2, tokens, share), BF16),
            pltpu.VMEM((2, tokens, share), BF16),
            pltpu.VMEM((2, tokens, share), BF16),
            pltpu.VMEM((2, tokens, share), F32),
            pltpu.VMEM((2, tokens, share), F32),
            pltpu.SemaphoreType.DMA((4,)),
            pltpu.SemaphoreType.DMA((2, 3)),
            pltpu.SemaphoreType.DMA((2, 3)),
        ],
        compiler_params=params(60, collective_id=0, has_side_effects=True),
        cost_estimate=pl.CostEstimate(flops=2 * size, bytes_accessed=100 * size, transcendentals=0),
        name="ring_all",
    )(*arrays, *extra)
    return out[:count], out[count], out[count + 1]


def dp_sum(arrays, n):
    return [
        lax.all_gather(
            lax.psum_scatter(a, "dp", scatter_dimension=0, tiled=True).astype(BF16), "dp", axis=0, tiled=True
        ).astype(F32)
        if a.shape[0] % n == 0
        else lax.psum(a, "dp")
        for a in arrays
    ]


PIECES = 4


def exchange(tokens, features, product, finish, fill_one, fill_two, out, scratch):
    core_send, core_recv, part, x_send, x_recv, low_send, send_sem, recv_sem, keep_sem = scratch
    at = lax.axis_index("tensor")
    core = lax.rem(at, 2)
    x = at // 2
    core_peer = x * 2 + 1 - core
    x_peer = (1 - x) * 2 + core
    block = tokens // 4
    rows = block // PIECES
    wide = features // 3
    barrier = pltpu.get_barrier_semaphore()
    for target in (core_peer, x_peer):
        pl.semaphore_signal(barrier, inc=1, device_id={"tensor": target}, device_id_type=MESH)
    pl.semaphore_wait(barrier, 2)

    def copy(kind, j, source, target, device):
        return pltpu.make_async_remote_copy(
            source, target, send_sem.at[kind, j], recv_sem.at[kind, j],
            device_id={"tensor": device}, device_id_type=MESH,
        )

    def place_of(c, xx, j):
        return pl.ds(pl.multiple_of((c * 2 + xx) * block + j * rows, rows), rows)

    def piece(j):
        return pl.ds(j * rows, rows)

    def term(c, xx, ref, kind):
        here = pl.ds(pl.multiple_of((c * 2 + xx) * block, block), block)
        for n in range(3):
            cols = pl.ds(n * wide, wide)
            ref[kind, :, cols] = product(here, cols).astype(ref.dtype)

    def core_copy(kind, j):
        return copy(kind, j, core_send.at[kind, piece(j)], core_recv.at[kind, piece(j)], core_peer)

    def x_copy(j):
        return copy(2, j, x_send.at[piece(j)], x_recv.at[piece(j)], x_peer)

    def low_copy(kind, j, c, xx, device):
        return copy(kind, j, low_send.at[piece(j)], out.at[place_of(c, xx, j)], device)

    def relay(j, c, xx):
        return copy(5, j, out.at[place_of(c, xx, j)], out.at[place_of(c, xx, j)], core_peer)

    def keep(j):
        return pltpu.make_async_copy(low_send.at[piece(j)], out.at[place_of(core, x, j)], keep_sem.at[j])

    term(1 - core, 1 - x, core_send, 0)
    for j in range(PIECES):
        core_copy(0, j).start()
    term(core, 1 - x, part, 0)
    for j in range(PIECES):
        core_copy(0, j).wait_recv()
        x_send[piece(j), :] = (part[0, piece(j), :] + core_recv[0, piece(j), :].astype(F32)).astype(BF16)
        x_copy(j).start()
    term(1 - core, x, core_send, 1)
    for j in range(PIECES):
        core_copy(1, j).start()
    term(core, x, part, 1)
    fill_one()
    for j in range(PIECES):
        core_copy(1, j).wait_recv()
        x_copy(j).wait_recv()
        here = piece(j)
        total = part[1, here, :] + core_recv[1, here, :].astype(F32) + x_recv[here, :].astype(F32)
        low_send[here, :] = finish(here, total)
        low_copy(3, j, core, x, x_peer).start()
        low_copy(4, j, core, x, core_peer).start()
        keep(j).start()
    fill_two()
    for j in range(PIECES):
        low_copy(3, j, core, 1 - x, x_peer).wait_recv()
        relay(j, core, 1 - x).start()
    for j in range(PIECES):
        low_copy(4, j, 1 - core, x, core_peer).wait_recv()
        relay(j, 1 - core, 1 - x).wait_recv()
        keep(j).wait()
        core_copy(0, j).wait_send()
        core_copy(1, j).wait_send()
        x_copy(j).wait_send()
        low_copy(3, j, core, x, x_peer).wait_send()
        low_copy(4, j, core, x, core_peer).wait_send()
        relay(j, core, 1 - x).wait_send()


def exchange_scratch(block, features):
    return [
        pltpu.VMEM((2, block, features), BF16),
        pltpu.VMEM((2, block, features), BF16),
        pltpu.VMEM((2, block, features), F32),
        pltpu.VMEM((block, features), BF16),
        pltpu.VMEM((block, features), BF16),
        pltpu.VMEM((block, features), BF16),
        pltpu.SemaphoreType.DMA((6, PIECES)),
        pltpu.SemaphoreType.DMA((6, PIECES)),
        pltpu.SemaphoreType.DMA((PIECES,)),
    ]


def project_kernel(mixed_ref, weight_ref, own_ref, gain_ref, two_out, resid_out, *scratch):
    def product(rows, cols):
        return jnp.dot(mixed_ref[rows, :], weight_ref[:, cols], preferred_element_type=F32)

    def finish(rows, total):
        resid = own_ref[rows, :].astype(F32) + total
        resid_out[rows, :] = resid
        return (resid * rsqrt_mean(resid) * gain_ref[...]).astype(BF16)

    def nothing():
        return None

    exchange(mixed_ref.shape[0], weight_ref.shape[1], product, finish, nothing, nothing, two_out, scratch)


def project(mixed_low, out_weight, own, gain):
    tokens = mixed_low.shape[0]
    features = out_weight.shape[1]
    block = tokens // 4
    return pl.pallas_call(
        project_kernel,
        in_specs=[pl.BlockSpec(memory_space=pltpu.VMEM)] * 4,
        out_specs=[pl.BlockSpec(memory_space=pl.ANY), pl.BlockSpec(memory_space=pltpu.VMEM)],
        out_shape=[
            jax.ShapeDtypeStruct((tokens, features), BF16),
            jax.ShapeDtypeStruct((block, features), F32),
        ],
        scratch_shapes=exchange_scratch(block, features),
        compiler_params=params(22, collective_id=1, has_side_effects=True),
        cost_estimate=pl.CostEstimate(flops=2 * mixed_low.size * features, bytes_accessed=tokens * features * 80, transcendentals=0),
        name="project",
    )(mixed_low, out_weight, own, gain)


def pull_kernel(
    gate_ref, up_ref, gate_w, up_w, two_ref, resid_ref, cot_ref, gain_ref,
    low_out, gain_out, gate_grad, up_grad, *scratch,
):
    features = gate_w.shape[0]
    step = 256
    gain_out[...] = jnp.zeros_like(gain_out)

    def product(rows, cols):
        return lax.dot_general(
            gate_ref[rows, :], gate_w[cols, :], (((1,), (1,)), ((), ())), preferred_element_type=F32
        ) + lax.dot_general(up_ref[rows, :], up_w[cols, :], (((1,), (1,)), ((), ())), preferred_element_type=F32)

    def finish(rows, total):
        resid = resid_ref[rows, :]
        q = rsqrt_mean(resid)
        gain_out[...] += column_total(total * resid * q)
        weighed = gain_ref[...] * total
        pulled = q * weighed - resid * q * q * q * jnp.mean(weighed * resid, axis=-1, keepdims=True)
        return (cot_ref[rows, :].astype(F32) + pulled).astype(BF16)

    def weight_grad(source, target):
        def run(n, carry):
            cols = pl.ds(pl.multiple_of(n * step, step), step)
            target[cols, :] = lax.dot_general(
                two_ref[:, cols], source[...], (((0,), (0,)), ((), ())), preferred_element_type=F32
            ).astype(BF16)
            return carry

        def go():
            lax.fori_loop(0, features // step, run, 0)

        return go

    exchange(
        gate_ref.shape[0], features, product, finish,
        weight_grad(gate_ref, gate_grad), weight_grad(up_ref, up_grad), low_out, scratch,
    )


def pull(d_gate, d_up, gate_w, up_w, two_low, resid, cot, gain):
    tokens, hidden = d_gate.shape
    features = gate_w.shape[0]
    block = tokens // 4
    vmem = pl.BlockSpec(memory_space=pltpu.VMEM)
    return pl.pallas_call(
        pull_kernel,
        in_specs=[vmem] * 8,
        out_specs=[pl.BlockSpec(memory_space=pl.ANY), vmem, vmem, vmem],
        out_shape=[
            jax.ShapeDtypeStruct((tokens, features), BF16),
            jax.ShapeDtypeStruct((1, features), F32),
            jax.ShapeDtypeStruct((features, hidden), BF16),
            jax.ShapeDtypeStruct((features, hidden), BF16),
        ],
        scratch_shapes=exchange_scratch(block, features),
        compiler_params=params(46, collective_id=2, has_side_effects=True),
        cost_estimate=pl.CostEstimate(flops=8 * d_gate.size * features, bytes_accessed=tokens * features * 80, transcendentals=0),
        name="pull",
    )(d_gate, d_up, gate_w, up_w, two_low, resid, cot, gain)


def rsqrt_mean(v):
    return lax.rsqrt(jnp.mean(v * v, axis=-1, keepdims=True) + EPSILON)


def dot(a, b, left, right):
    return lax.dot_general(a, b, (((left,), (right,)), ((), ())), preferred_element_type=F32)


def body(
    n_dp,
    inputs,
    segment_ids,
    cotangent,
    first_gain,
    gate_weight,
    gate_bias,
    branch_weight,
    branch_bias,
    conv_weight,
    conv_bias,
    rate_weight,
    rate_bias,
    input_weight,
    input_bias,
    decay_param,
    out_weight,
    second_gain,
    ffn_gate,
    ffn_up,
    ffn_down,
):
    tokens, share = inputs.shape
    features = share * 4
    channels = gate_weight.shape[1]
    gain_one = first_gain.astype(F32)
    gain_two = second_gain.astype(F32)
    at = lax.axis_index("tensor")
    start = token_start(tokens)
    block = tokens // 4

    row = jnp.arange(tokens, dtype=jnp.int32)
    masks = []
    for k in range(4):
        offset = max(k, 1)
        earlier = jnp.concatenate([jnp.full((offset,), -1, jnp.int32), segment_ids[:-offset]])
        same = (row >= offset) & (segment_ids == earlier)
        masks.append(same if k else ~same)
    masks = jnp.pad(jnp.stack(masks, axis=1).astype(F32), ((0, HALO), (0, 0)))
    rows = jnp.concatenate(
        [
            conv_weight.astype(F32),
            jnp.concatenate([conv_bias, rate_bias, input_bias]).astype(F32).reshape(3, channels),
            jax.nn.softplus(-decay_param)[None],
        ]
    )

    across, masks, rows, gate_bias, branch_bias, gain_one, gain_two = lax.optimization_barrier(
        (swap_x(inputs), masks, rows, gate_bias.astype(F32), branch_bias.astype(F32), gain_one, gain_two)
    )
    in_pieces = (inputs, swap_core(inputs), across, swap_core(across))
    later_cot, _ = lax.optimization_barrier((cotangent, across))
    cot_across = swap_x(later_cot)
    whole_in = join_features(in_pieces)
    in_f = whole_in.astype(F32)
    q_one = rsqrt_mean(in_f)
    normed_low = lax.optimization_barrier((in_f * q_one * gain_one).astype(BF16))
    gate_pre = dot(normed_low, gate_weight, 1, 0) + gate_bias.astype(F32)
    branch_pre = dot(normed_low, branch_weight, 1, 0) + branch_bias.astype(F32)
    conv, rate, opened, state, mixed_low = forward_block(
        gate_pre, branch_pre, masks, rows, rate_weight, input_weight
    )
    mixed_low, cot_across = lax.optimization_barrier((mixed_low, cot_across))
    whole_cot = join_features((cotangent, swap_core(cotangent), cot_across, swap_core(cot_across)))
    two_low, resid = project(
        mixed_low, out_weight, lax.dynamic_slice_in_dim(whole_in, start, block, 0), gain_two[None]
    )
    d_hidden = dot(whole_cot, ffn_down, 1, 1)
    hidden_gate = dot(two_low, ffn_gate, 1, 0)
    hidden_up = dot(two_low, ffn_up, 1, 0)
    hidden_act, hidden_slope = gelu_parts(hidden_gate)
    hidden_low = (hidden_act * hidden_up).astype(BF16)
    cut = hidden_low.shape[1] * 4 // 9
    down_early = dot(hidden_low[:, :cut], whole_cot, 0, 0)
    down_late = dot(hidden_low[:, cut:], whole_cot, 0, 0)
    d_hgate = (d_hidden * hidden_up * hidden_slope).astype(BF16)
    d_hup = (d_hidden * hidden_act).astype(BF16)
    if n_dp == 8:
        down_early, down_late, d_hgate, d_hup = lax.optimization_barrier(
            (down_early.astype(BF16), down_late.astype(BF16), d_hgate, d_hup)
        )
        down_early = lax.psum(down_early, "dp")
    cot_mine = lax.dynamic_slice_in_dim(whole_cot, start, block, 0)
    d_resid_low, second_gain_grad, ffn_gate_grad, ffn_up_grad = pull(
        d_hgate, d_hup, ffn_gate, ffn_up, two_low, resid, cot_mine, gain_two[None]
    )
    second_gain_grad = second_gain_grad[0]
    out_weight_grad = dot(mixed_low, d_resid_low, 0, 0)
    d_mixed = dot(d_resid_low, out_weight, 1, 1)
    d_gate_low, d_branch_low, misc = backward_block(
        d_mixed, gate_pre, branch_pre, conv, rate, opened, state, masks, rows, rate_weight, input_weight
    )
    if n_dp == 8:
        down_early, down_late, d_gate_low = lax.optimization_barrier((down_early, down_late, d_gate_low))
        down_late = lax.psum(down_late, "dp")
    gate_weight_grad = dot(normed_low, d_gate_low, 0, 0)
    branch_weight_grad = dot(normed_low, d_branch_low, 0, 0)
    first_share = dot(d_gate_low, gate_weight, 1, 1) + dot(d_branch_low, branch_weight, 1, 1)
    product = first_share * in_f
    sums = jnp.concatenate([
        jnp.sum(product * q_one, axis=0), second_gain_grad, jnp.sum(product * gain_one, axis=1)
    ])
    sums = tensor_sum(sums.reshape(-1, LANES)).reshape(-1)
    gains = sums[: 2 * features].reshape(-1, channels)
    mean_one = sums[2 * features :, None] / features
    misc = lax.dynamic_update_slice_in_dim(misc, gains.astype(BF16), 2 * LANES + 16, 0)
    summed = [ffn_gate_grad, ffn_up_grad, gate_weight_grad, branch_weight_grad, out_weight_grad, misc]
    if n_dp == 8:
        summed, output, d_first = ring_all([a.astype(BF16) for a in summed], hidden_low, ffn_down, resid, first_share)
        (*summed, down_late) = lax.optimization_barrier((*summed, down_late))
        summed = [a.astype(F32) for a in (jnp.concatenate([down_early, down_late]), *summed)]
    else:
        summed = dp_sum([jnp.concatenate([down_early, down_late]), *summed], n_dp)
        first_here, first_there = scatter_features(first_share)
        d_first = first_here + first_there.astype(F32)
        ffn_part = dot(hidden_low, ffn_down, 1, 0)
        with_resid = lax.dynamic_slice_in_dim(ffn_part, start, block, 0) + resid
        ffn_part = lax.dynamic_update_slice_in_dim(ffn_part, with_resid, start, 0)
        output_here, output_there = scatter_features(ffn_part)
        output = (output_here + output_there.astype(F32)).astype(BF16)
    ffn_down_grad, ffn_gate_grad, ffn_up_grad, gate_weight_grad, branch_weight_grad, out_weight_grad, misc = summed

    own_in = inputs.astype(F32)
    own_gain = lax.dynamic_slice_in_dim(gain_one, at * share, share, 0)
    input_grad = (
        lax.dynamic_slice_in_dim(d_resid_low, at * share, share, 1).astype(F32)
        + q_one * own_gain * d_first
        - own_in * q_one * q_one * q_one * mean_one
    )
    heads = rate_weight.shape[0]

    def blocks(v):
        return v.reshape(LANES, heads, LANES).transpose(1, 0, 2)

    small = misc[2 * LANES : 2 * LANES + 16]
    gains = misc[2 * LANES + 16 : 2 * LANES + 16 + gains.shape[0]].reshape(2, features)
    decay_grad = -small[7] * jax.nn.sigmoid(-decay_param)
    return (
        output,
        input_grad,
        gains[0],
        gate_weight_grad,
        small[8],
        branch_weight_grad,
        small[9],
        small[0:4],
        small[4],
        blocks(misc[:LANES]),
        small[5],
        blocks(misc[LANES : 2 * LANES]),
        small[6],
        decay_grad,
        out_weight_grad,
        gains[1],
        ffn_gate_grad,
        ffn_up_grad,
        ffn_down_grad,
    )


def solution(mesh):
    in_specs = (
        P("dp", "tensor"),
        P("dp"),
        P("dp", "tensor"),
        P(),
        P(None, "tensor"),
        P("tensor"),
        P(None, "tensor"),
        P("tensor"),
        P(None, "tensor"),
        P("tensor"),
        P("tensor", None, None),
        P("tensor"),
        P("tensor", None, None),
        P("tensor"),
        P("tensor"),
        P("tensor", None),
        P(),
        P(None, "tensor"),
        P(None, "tensor"),
        P("tensor", None),
    )
    out_specs = (
        P("dp", "tensor"),
        P("dp", "tensor"),
        P(),
        P(None, "tensor"),
        P("tensor"),
        P(None, "tensor"),
        P("tensor"),
        P(None, "tensor"),
        P("tensor"),
        P("tensor", None, None),
        P("tensor"),
        P("tensor", None, None),
        P("tensor"),
        P("tensor"),
        P("tensor", None),
        P(),
        P(None, "tensor"),
        P(None, "tensor"),
        P("tensor", None),
    )
    return jax.shard_map(
        functools.partial(body, mesh.shape["dp"]), mesh=mesh, in_specs=in_specs, out_specs=out_specs, check_vma=False
    )
```

```python
import functools

import jax
import jax.numpy as jnp
from jax import lax
from jax.experimental import pallas as pl
from jax.experimental.pallas import tpu as pltpu
from jax.sharding import PartitionSpec as P

EPSILON = 1e-06
FLOOR = 0.05
F32 = jnp.float32
BF16 = jnp.bfloat16
LANES = 128
SPAN = 32
HALO = 8
MIB = 1024 * 1024


def params(mib, **more):
    return pltpu.CompilerParams(vmem_limit_bytes=mib * MIB, **more)


def gelu_parts(v):
    c0 = 0.7978845608028654
    c1 = 0.044715
    t = jnp.tanh(c0 * (v + c1 * v * v * v))
    act = 0.5 * v * (1.0 + t)
    slope = 0.5 * (1.0 + t) + 0.5 * v * (1.0 - t * t) * c0 * (1.0 + 3.0 * c1 * v * v)
    return act, slope


def sigmoid(v):
    return 0.5 * jnp.tanh(0.5 * v) + 0.5


def shift_down(v, amount, fill):
    row = lax.broadcasted_iota(jnp.int32, v.shape, 0)
    return jnp.where(row >= amount, pltpu.roll(v, amount, 0), fill)


def shift_up(v, amount, fill):
    row = lax.broadcasted_iota(jnp.int32, v.shape, 0)
    size = v.shape[0]
    return jnp.where(row < size - amount, pltpu.roll(v, size - amount, 0), fill)


def scale_of(decayed, reset):
    rest = 1.0 - decayed * decayed
    return jnp.where(reset, 1.0, jnp.sqrt(jnp.maximum(rest, FLOOR))), rest


def forward_kernel(
    gate_ref, branch_ref, mask_ref, row_ref, rate_w, input_w,
    conv_out, rate_out, open_out, state_out, mixed_out, padded, keep_s, local_s,
):
    tokens = gate_ref.shape[0]
    step = 128
    spans = tokens // SPAN
    padded[0:HALO, :] = jnp.zeros((HALO, LANES), F32)
    padded[HALO:, :] = branch_ref[...]
    wr = rate_w[0]
    wi = input_w[0]

    def fill(i, carry):
        r0 = pl.multiple_of(i * step, step)
        here = pl.ds(r0, step)
        wide = padded[pl.ds(r0, step + HALO), :]
        total = row_ref[4:5, :] + row_ref[0:1, :] * wide[HALO:, :]
        for k in range(1, 4):
            total = total + row_ref[k : k + 1, :] * wide[HALO - k : HALO - k + step, :] * mask_ref[here, k : k + 1]
        low = total.astype(BF16)
        rate = sigmoid(jnp.dot(low, wr, preferred_element_type=F32) + row_ref[5:6, :])
        opened = sigmoid(jnp.dot(low, wi, preferred_element_type=F32) + row_ref[6:7, :])
        reset = mask_ref[here, 0:1] > 0.5
        decayed = jnp.exp(-8.0 * rate * row_ref[7:8, :])
        scale, _ = scale_of(decayed, reset)
        conv_out[here, :] = total
        rate_out[here, :] = rate
        open_out[here, :] = opened
        keep_s[here, :] = jnp.where(reset, 0.0, decayed)
        state_out[here, :] = scale * opened * total
        return carry

    lax.fori_loop(0, tokens // step, fill, 0)
    h = jnp.zeros((spans, LANES), F32)
    p = jnp.ones((spans, LANES), F32)
    for k in range(SPAN):
        at = pl.ds(k, spans, stride=SPAN)
        a = keep_s[at, :]
        h = a * h + state_out[at, :]
        p = p * a
        local_s[at, :] = h
        keep_s[at, :] = p
    jump = 1
    while jump < spans:
        h = h + p * shift_down(h, jump, 0.0)
        p = p * shift_down(p, jump, 1.0)
        jump *= 2
    carry_in = shift_down(h, 1, 0.0)
    for k in range(SPAN):
        at = pl.ds(k, spans, stride=SPAN)
        state_out[at, :] = local_s[at, :] + keep_s[at, :] * carry_in

    def mix(i, carry):
        here = pl.ds(pl.multiple_of(i * step, step), step)
        act, _ = gelu_parts(gate_ref[here, :])
        mixed_out[here, :] = (act * state_out[here, :]).astype(BF16)
        return carry

    lax.fori_loop(0, tokens // step, mix, 0)


def forward_block(gate_pre, branch_pre, masks, rows, rate_weight, input_weight):
    tokens, channels = gate_pre.shape
    heads = rate_weight.shape[0]
    col = pl.BlockSpec((tokens, LANES), lambda h: (0, h))
    whole = pl.BlockSpec(masks.shape, lambda h: (0, 0))
    table = pl.BlockSpec((8, LANES), lambda h: (0, h))
    square = pl.BlockSpec((1, LANES, LANES), lambda h: (h, 0, 0))
    full = jax.ShapeDtypeStruct((tokens, channels), F32)
    return pl.pallas_call(
        forward_kernel,
        grid=(heads,),
        in_specs=[col, col, whole, table, square, square],
        out_specs=[col] * 5,
        out_shape=[full] * 4 + [jax.ShapeDtypeStruct((tokens, channels), BF16)],
        scratch_shapes=[
            pltpu.VMEM((tokens + HALO, LANES), F32),
            pltpu.VMEM((tokens, LANES), F32),
            pltpu.VMEM((tokens, LANES), F32),
        ],
        compiler_params=params(60),
        cost_estimate=pl.CostEstimate(flops=tokens * channels * 700, bytes_accessed=tokens * channels * 26, transcendentals=tokens * channels * 5),
        name="recurrence_forward",
    )(gate_pre, branch_pre, masks, rows, rate_weight, input_weight)


def column_total(v):
    return jnp.sum(v, axis=0, keepdims=True)


def backward_kernel(
    dmix_ref, gate_ref, branch_ref, conv_ref, rate_ref, open_ref, state_ref, mask_ref, row_ref, rate_w, input_w,
    dgate_out, dbranch_out, misc_out, padded, keep_s, adj_s, dconv_s, prev_s, rate_g, input_g, small_g,
):
    tokens = gate_ref.shape[0]
    step = 128
    count = tokens // step
    spans = tokens // SPAN
    zero_halo = jnp.zeros((HALO, LANES), F32)
    padded[0:HALO, :] = zero_halo
    padded[HALO:, :] = branch_ref[...]
    prev_s[0:HALO, :] = zero_halo
    prev_s[HALO:, :] = state_ref[...]
    keep_s[tokens:, :] = zero_halo
    dconv_s[tokens:, :] = zero_halo
    wr = rate_w[0]
    wi = input_w[0]

    def fill(i, total):
        here = pl.ds(pl.multiple_of(i * step, step), step)
        act, slope = gelu_parts(gate_ref[here, :])
        dmix = dmix_ref[here, :]
        dgate = (dmix * state_ref[here, :] * slope).astype(BF16)
        dgate_out[here, :] = dgate
        adj_s[here, :] = dmix * act
        reset = mask_ref[here, 0:1] > 0.5
        keep_s[here, :] = jnp.where(reset, 0.0, jnp.exp(-8.0 * rate_ref[here, :] * row_ref[7:8, :]))
        return total + column_total(dgate.astype(F32))

    gate_bias = lax.fori_loop(0, count, fill, jnp.zeros((1, LANES), F32))
    h = jnp.zeros((spans, LANES), F32)
    p = jnp.ones((spans, LANES), F32)
    for k in reversed(range(SPAN)):
        at = pl.ds(k, spans, stride=SPAN)
        a = keep_s[pl.ds(k + 1, spans, stride=SPAN), :]
        h = a * h + adj_s[at, :]
        p = p * a
        adj_s[at, :] = h
        dconv_s[at, :] = p
    jump = 1
    while jump < spans:
        h = h + p * shift_up(h, jump, 0.0)
        p = p * shift_up(p, jump, 1.0)
        jump *= 2
    carry_in = shift_up(h, 1, 0.0)
    for k in range(SPAN):
        at = pl.ds(k, spans, stride=SPAN)
        adj_s[at, :] = adj_s[at, :] + dconv_s[at, :] * carry_in

    nothing = jnp.zeros((1, LANES), F32)
    rate_g[...] = jnp.zeros_like(rate_g)
    input_g[...] = jnp.zeros_like(input_g)

    def gates(i, totals):
        r0 = pl.multiple_of(i * step, step)
        here = pl.ds(r0, step)
        adj = adj_s[here, :]
        conv = conv_ref[here, :]
        rate = rate_ref[here, :]
        opened = open_ref[here, :]
        reset = mask_ref[here, 0:1] > 0.5
        decay_row = row_ref[7:8, :]
        decayed = jnp.exp(-8.0 * rate * decay_row)
        scale, rest = scale_of(decayed, reset)
        before = prev_s[pl.ds(r0, step + HALO), :][HALO - 1 : HALO - 1 + step, :]
        pull = jnp.where(rest > FLOOR, 1.0, jnp.where(rest == FLOOR, 0.5, 0.0))
        d_scale = adj * opened * conv
        d_decayed = jnp.where(reset, 0.0, adj * before - d_scale * pull * decayed / scale)
        d_log = d_decayed * decayed * -8.0
        d_rate = (d_log * decay_row * rate * (1.0 - rate)).astype(BF16)
        d_input = (adj * scale * conv * opened * (1.0 - opened)).astype(BF16)
        d_conv = (
            adj * scale * opened
            + lax.dot_general(d_rate, wr, (((1,), (1,)), ((), ())), preferred_element_type=F32)
            + lax.dot_general(d_input, wi, (((1,), (1,)), ((), ())), preferred_element_type=F32)
        )
        dconv_s[here, :] = d_conv
        low = conv.astype(BF16)
        rate_g[...] += lax.dot_general(low, d_rate, (((0,), (0,)), ((), ())), preferred_element_type=F32)
        input_g[...] += lax.dot_general(low, d_input, (((0,), (0,)), ((), ())), preferred_element_type=F32)
        wide = padded[pl.ds(r0, step + HALO), :]
        news = [
            column_total(d_conv * wide[HALO:, :]),
            *[
                column_total(d_conv * mask_ref[here, k : k + 1] * wide[HALO - k : HALO - k + step, :])
                for k in range(1, 4)
            ],
            column_total(d_conv),
            column_total(d_rate.astype(F32)),
            column_total(d_input.astype(F32)),
            column_total(d_log * rate),
        ]
        return tuple(t + n for t, n in zip(totals, news))

    totals = lax.fori_loop(0, count, gates, (nothing,) * 8)

    def conv_back(i, total):
        r0 = pl.multiple_of(i * step, step)
        here = pl.ds(r0, step)
        wide = dconv_s[pl.ds(r0, step + HALO), :]
        d_branch = row_ref[0:1, :] * wide[:step, :]
        for k in range(1, 4):
            part = wide * mask_ref[pl.ds(r0, step + HALO), k : k + 1]
            d_branch = d_branch + row_ref[k : k + 1, :] * part[k : k + step, :]
        low = d_branch.astype(BF16)
        dbranch_out[here, :] = low
        return total + column_total(low.astype(F32))

    branch_bias = lax.fori_loop(0, count, conv_back, nothing)
    small_g[...] = jnp.zeros_like(small_g)
    for at, value in enumerate((*totals, gate_bias, branch_bias)):
        small_g[at : at + 1, :] = value
    misc_out[...] = jnp.zeros_like(misc_out)
    misc_out[0:LANES, :] = rate_g[...].astype(BF16)
    misc_out[LANES : 2 * LANES, :] = input_g[...].astype(BF16)
    misc_out[2 * LANES : 2 * LANES + 16, :] = small_g[...].astype(BF16)


def backward_block(d_mixed, gate_pre, branch_pre, conv, rate, opened, state, masks, rows, rate_weight, input_weight):
    tokens, channels = gate_pre.shape
    heads = rate_weight.shape[0]
    col = pl.BlockSpec((tokens, LANES), lambda h: (0, h))
    whole = pl.BlockSpec(masks.shape, lambda h: (0, 0))
    table = pl.BlockSpec((8, LANES), lambda h: (0, h))
    square = pl.BlockSpec((1, LANES, LANES), lambda h: (h, 0, 0))
    misc = pl.BlockSpec((3 * LANES, LANES), lambda h: (0, h))
    return pl.pallas_call(
        backward_kernel,
        grid=(heads,),
        in_specs=[col] * 7 + [whole, table, square, square],
        out_specs=[col, col, misc],
        out_shape=[
            jax.ShapeDtypeStruct((tokens, channels), BF16),
            jax.ShapeDtypeStruct((tokens, channels), BF16),
            jax.ShapeDtypeStruct((3 * LANES, channels), BF16),
        ],
        scratch_shapes=[
            pltpu.VMEM((tokens + HALO, LANES), F32),
            pltpu.VMEM((tokens + HALO, LANES), F32),
            pltpu.VMEM((tokens, LANES), F32),
            pltpu.VMEM((tokens + HALO, LANES), F32),
            pltpu.VMEM((tokens + HALO, LANES), F32),
            pltpu.VMEM((LANES, LANES), F32),
            pltpu.VMEM((LANES, LANES), F32),
            pltpu.VMEM((16, LANES), F32),
        ],
        compiler_params=params(60),
        cost_estimate=pl.CostEstimate(flops=tokens * channels * 1400, bytes_accessed=tokens * channels * 32, transcendentals=tokens * channels * 5),
        name="recurrence_backward",
    )(d_mixed, gate_pre, branch_pre, conv, rate, opened, state, masks, rows, rate_weight, input_weight)


X_PAIRS = [(0, 2), (2, 0), (1, 3), (3, 1)]
CORE_PAIRS = [(0, 1), (1, 0), (2, 3), (3, 2)]


def swap_x(v):
    return lax.ppermute(v, "tensor", X_PAIRS)


def swap_core(v):
    return lax.ppermute(v, "tensor", CORE_PAIRS)


def place():
    at = lax.axis_index("tensor")
    return at // 2, at % 2


def share_features(v):
    across = swap_x(v)
    return v, swap_core(v), across, swap_core(across)


def join_features(pieces):
    at = lax.axis_index("tensor")
    rows, share = pieces[0].shape
    out = jnp.zeros((rows, share * 4), pieces[0].dtype)
    for distance, piece in enumerate(pieces):
        out = lax.dynamic_update_slice_in_dim(out, piece, (at ^ distance) * share, 1)
    return out


def token_start(tokens):
    x, core = place()
    return (core * 2 + x) * (tokens // 4)


def scatter_tokens(v):
    x, core = place()
    half = v.shape[0] // 2
    mine = lax.dynamic_slice_in_dim(v, core * half, half, 0)
    other = lax.dynamic_slice_in_dim(v, (1 - core) * half, half, 0)
    both = mine + swap_core(other.astype(BF16)).astype(F32)
    quarter = half // 2
    mine = lax.dynamic_slice_in_dim(both, x * quarter, quarter, 0)
    other = lax.dynamic_slice_in_dim(both, (1 - x) * quarter, quarter, 0)
    return mine + swap_x(other.astype(BF16)).astype(F32)


def gather_tokens(v):
    x, core = place()
    block = v.shape[0]
    across = swap_x(v)
    near = swap_core(v)
    far = swap_core(across)
    out = jnp.zeros((block * 4, v.shape[1]), v.dtype)
    for piece, where in (
        (v, core * 2 + x),
        (near, (1 - core) * 2 + x),
        (across, core * 2 + 1 - x),
        (far, (1 - core) * 2 + 1 - x),
    ):
        out = lax.dynamic_update_slice_in_dim(out, piece, where * block, 0)
    return out


def scatter_features(v):
    x, core = place()
    share = v.shape[1] // 4

    def part(at):
        return lax.dynamic_slice_in_dim(v, at * share, share, 1)

    def pair(c):
        return part(x * 2 + c), part((1 - x) * 2 + c)

    mine, other = pair(core)
    send_mine, send_other = pair(1 - core)
    got_mine = swap_core(send_mine.astype(BF16)).astype(F32)
    got_other = swap_core(send_other.astype(BF16)).astype(F32)
    return mine + got_mine, swap_x((other + got_other).astype(BF16))


def tensor_sum(v):
    v = v + swap_core(v)
    return v + swap_x(v)


MESH = pl.DeviceIdType.MESH
HELD = 9


def ring_kernel(given, n, *refs):
    count = given + 3
    ins, extra, refs = refs[:given], refs[given : given + HELD], refs[given + HELD :]
    outs, sums, refs = refs[:count], refs[count : count + 2], refs[count + 2 :]
    slots, locals_, refs = refs[:count], refs[count : 2 * count], refs[2 * count :]
    send_sem, recv_sem, load_sem, keep_sem = refs[:4]
    held, refs = refs[4 : 4 + HELD], refs[4 + HELD :]
    core_send, core_recv, x_send, x_recv, own, other, held_sem, share_send, share_recv = refs[:9]
    made = refs[9:]
    ins = (*ins, *made)
    normed_s, gate_s, branch_s, mixed_s, low_s, hidden_s, down_s, resid_s, first_s = held
    me = lax.axis_index("dp")
    y = lax.rem(me, 2)
    z = me // 2
    p = jnp.where(y == 0, z, n - 1 - z)

    def device(at):
        return jnp.where(at < n // 2, 2 * at, 2 * (n - 1 - at) + 1)

    after, before = device(lax.rem(p + 1, n)), device(lax.rem(p + n - 1, n))
    targets = (after, before)
    at = lax.axis_index("tensor")
    core = lax.rem(at, 2)
    x = at // 2
    core_peer = x * 2 + 1 - core
    x_peer = (1 - x) * 2 + core
    barrier = pltpu.get_barrier_semaphore()
    for target in targets:
        pl.semaphore_signal(barrier, inc=1, device_id={"dp": target}, device_id_type=MESH)
    for target in (core_peer, x_peer):
        pl.semaphore_signal(barrier, inc=1, device_id={"tensor": target}, device_id_type=MESH)
    pl.semaphore_wait(barrier, 4)

    def hold(i):
        return pltpu.make_async_copy(extra[i], held[i], held_sem.at[i])

    tokens, share = own.shape
    block = tokens // 4

    def share_copy(kind, i):
        if i < 2:
            source, target, device = core_send.at[kind, i], core_recv.at[kind, i], core_peer
        else:
            source, target, device = x_send.at[kind], x_recv.at[kind], x_peer
        return pltpu.make_async_remote_copy(
            source, target, share_send.at[kind, i], share_recv.at[kind, i],
            device_id={"tensor": device}, device_id_type=MESH,
        )

    def share_cols(xx, c):
        return pl.ds(pl.multiple_of((xx * 2 + c) * share, LANES), share)

    def output_terms(b):
        rows = pl.ds(b * block, block)
        mine = jnp.where(core * 2 + x == b, 1.0, 0.0)
        for xx, c, ref in (
            (1 - x, 1 - core, core_send.at[0, 1]),
            (x, 1 - core, core_send.at[0, 0]),
            (1 - x, core, other),
            (x, core, own),
        ):
            cols = share_cols(xx, c)
            term = jnp.dot(hidden_s[rows, :], down_s[:, cols], preferred_element_type=F32) + mine * resid_s[:, cols]
            ref[rows, :] = term.astype(ref.dtype)

    def first_terms():
        core_send[1, 1] = first_s[:, share_cols(1 - x, 1 - core)].astype(BF16)
        core_send[1, 0] = first_s[:, share_cols(x, 1 - core)].astype(BF16)

    def share_start(kind):
        share_copy(kind, 1).start()
        share_copy(kind, 0).start()

    def share_forward(kind):
        share_copy(kind, 1).wait_recv()
        far = first_s[:, share_cols(1 - x, core)] if kind else other[...]
        x_send[kind] = (far + core_recv[kind, 1].astype(F32)).astype(BF16)
        share_copy(kind, 2).start()

    def share_finish(kind):
        share_copy(kind, 0).wait_recv()
        share_copy(kind, 2).wait_recv()
        near = first_s[:, share_cols(x, core)] if kind else own[...]
        total = near + core_recv[kind, 0].astype(F32) + x_recv[kind].astype(F32)
        sums[kind][...] = total.astype(sums[kind].dtype)

    def weight_grad(source, by, target):
        def run(i, carry):
            cols = pl.ds(pl.multiple_of(i * 256, 256), 256)
            target[cols, :] = lax.dot_general(
                source[:, cols], by[...], (((0,), (0,)), ((), ())), preferred_element_type=F32
            ).astype(BF16)
            return carry

        lax.fori_loop(0, source.shape[1] // 256, run, 0)

    def piece(ref, q, side, chunk):
        rows = ref.shape[0] // (2 * n)
        start = pl.multiple_of((2 * lax.rem(chunk + n, n) + side) * rows, 8)
        return ref.at[pl.ds(start, rows), :]

    def arriving(side, s):
        if s < n - 1:
            return p - 1 - s if side == 0 else p + 1 + s
        s -= n - 1
        return p - s if side == 0 else p + s

    def send(q, side, s, source):
        if s < n - 1:
            target = slots[q].at[s, side]
        else:
            chunk = p + 1 - (s - n + 1) if side == 0 else p - 1 + (s - n + 1)
            target = piece(outs[q], q, side, chunk + n)
        copy = pltpu.make_async_remote_copy(
            source, target, send_sem.at[q, side, s], recv_sem.at[q, side, s],
            device_id={"dp": targets[side]}, device_id_type=MESH,
        )
        copy.start()

    def wait(q, side, s, which):
        if s < n - 1:
            shape = slots[q].at[s, side]
        else:
            shape = piece(outs[q], q, side, arriving(side, s) + n)
        copy = pltpu.make_async_remote_copy(
            shape, shape, send_sem.at[q, side, s], recv_sem.at[q, side, s],
            device_id={"dp": targets[side]}, device_id_type=MESH,
        )
        (copy.wait_recv if which else copy.wait_send)()

    def load(q, side, s):
        return pltpu.make_async_copy(
            piece(ins[q], q, side, arriving(side, s) + n), locals_[q].at[s % 2, side], load_sem.at[q, side, s % 2]
        )

    def begin(q):
        for side in range(2):
            send(q, side, 0, piece(ins[q], q, side, p + n))
            load(q, side, 0).start()

    for q in range(given):
        begin(q)
    for i in range(HELD):
        hold(i).start()
    for i in range(5):
        hold(i).wait()
    for i, (source, by) in enumerate(((normed_s, gate_s), (normed_s, branch_s), (mixed_s, low_s))):
        weight_grad(source, by, made[i])
        begin(given + i)
    for i in range(5, HELD):
        hold(i).wait()
    for s in range(n - 1):
        if s == 1:
            share_start(0)
            first_terms()
            share_start(1)
        if s == 2:
            share_forward(0)
        if s == 3:
            share_forward(1)
        if s == 5:
            share_finish(0)
        if s == 6:
            share_finish(1)
        for q in range(count):
            if s == 0 and q < 4:
                output_terms(q)
            for side in range(2):
                if s + 1 < n - 1:
                    load(q, side, s + 1).start()
                load(q, side, s).wait()
                wait(q, side, s, True)
                slot = slots[q].at[s, side]
                slot[...] = (slot[...].astype(F32) + locals_[q][s % 2, side].astype(F32)).astype(BF16)
                send(q, side, s + 1, slot)
                if s == n - 2:
                    chunk = p + 1 if side == 0 else p - 1
                    pltpu.make_async_copy(slot, piece(outs[q], q, side, chunk + n), keep_sem.at[q, side]).start()
    for s in range(n - 1, 2 * n - 2):
        for q in range(count):
            for side in range(2):
                wait(q, side, s, True)
                if s + 1 < 2 * n - 2:
                    send(q, side, s + 1, piece(outs[q], q, side, arriving(side, s) + n))
    for q in range(count):
        for side in range(2):
            slot = slots[q].at[n - 2, side]
            chunk = p + 1 if side == 0 else p - 1
            pltpu.make_async_copy(slot, piece(outs[q], q, side, chunk + n), keep_sem.at[q, side]).wait()
            for s in range(2 * n - 2):
                wait(q, side, s, False)
    for kind in range(2):
        for i in range(3):
            share_copy(kind, i).wait_send()


def ring_all(arrays, normed, d_gate, d_branch, mixed, low, hidden, down, resid, first):
    n = 8
    given = len(arrays)
    made = [
        jax.ShapeDtypeStruct((a.shape[1], b.shape[1]), BF16)
        for a, b in ((normed, d_gate), (normed, d_branch), (mixed, low))
    ]
    reduced = [*arrays, *made]
    count = len(reduced)
    halves = [(a.shape[0] // (2 * n), a.shape[1]) for a in reduced]
    size = sum(a.size for a in reduced)
    extra = (normed, d_gate, d_branch, mixed, low, hidden, down, resid, first)
    tokens = hidden.shape[0]
    share = down.shape[1] // 4
    hbm = pl.BlockSpec(memory_space=pl.ANY)
    out = pl.pallas_call(
        functools.partial(ring_kernel, given, n),
        in_specs=[hbm] * (given + HELD),
        out_specs=[hbm] * count + [pl.BlockSpec(memory_space=pltpu.VMEM)] * 2,
        out_shape=[
            *[jax.ShapeDtypeStruct(a.shape, BF16) for a in reduced],
            jax.ShapeDtypeStruct((tokens, share), BF16),
            jax.ShapeDtypeStruct((tokens, share), F32),
        ],
        scratch_shapes=[
            *[pltpu.VMEM((n - 1, 2, *h), BF16) for h in halves],
            *[pltpu.VMEM((2, 2, *h), BF16) for h in halves],
            pltpu.SemaphoreType.DMA((count, 2, 2 * n - 2)),
            pltpu.SemaphoreType.DMA((count, 2, 2 * n - 2)),
            pltpu.SemaphoreType.DMA((count, 2, 2)),
            pltpu.SemaphoreType.DMA((count, 2)),
            *[pltpu.VMEM(a.shape, a.dtype) for a in extra],
            pltpu.VMEM((2, 2, tokens, share), BF16),
            pltpu.VMEM((2, 2, tokens, share), BF16),
            pltpu.VMEM((2, tokens, share), BF16),
            pltpu.VMEM((2, tokens, share), BF16),
            pltpu.VMEM((tokens, share), F32),
            pltpu.VMEM((tokens, share), F32),
            pltpu.SemaphoreType.DMA((HELD,)),
            pltpu.SemaphoreType.DMA((2, 3)),
            pltpu.SemaphoreType.DMA((2, 3)),
            *[pltpu.VMEM(a.shape, BF16) for a in made],
        ],
        compiler_params=params(63, collective_id=0, has_side_effects=True),
        cost_estimate=pl.CostEstimate(flops=2 * size, bytes_accessed=100 * size, transcendentals=0),
        name="ring_all",
    )(*arrays, *extra)
    return out[:count], out[count], out[count + 1]


def dp_sum(arrays, n):
    return [
        lax.all_gather(
            lax.psum_scatter(a, "dp", scatter_dimension=0, tiled=True).astype(BF16), "dp", axis=0, tiled=True
        ).astype(F32)
        if a.shape[0] % n == 0
        else lax.psum(a, "dp")
        for a in arrays
    ]


PIECES = 4


def exchange(tokens, features, product, finish, fill_one, fill_two, out, scratch):
    core_send, core_recv, part, x_send, x_recv, low_send, send_sem, recv_sem, keep_sem = scratch
    at = lax.axis_index("tensor")
    core = lax.rem(at, 2)
    x = at // 2
    core_peer = x * 2 + 1 - core
    x_peer = (1 - x) * 2 + core
    block = tokens // 4
    rows = block // PIECES
    wide = features // 3
    barrier = pltpu.get_barrier_semaphore()
    for target in (core_peer, x_peer):
        pl.semaphore_signal(barrier, inc=1, device_id={"tensor": target}, device_id_type=MESH)
    pl.semaphore_wait(barrier, 2)

    def copy(kind, j, source, target, device):
        return pltpu.make_async_remote_copy(
            source, target, send_sem.at[kind, j], recv_sem.at[kind, j],
            device_id={"tensor": device}, device_id_type=MESH,
        )

    def place_of(c, xx, j):
        return pl.ds(pl.multiple_of((c * 2 + xx) * block + j * rows, rows), rows)

    def piece(j):
        return pl.ds(j * rows, rows)

    def term(c, xx, ref, kind):
        here = pl.ds(pl.multiple_of((c * 2 + xx) * block, block), block)
        for n in range(3):
            cols = pl.ds(n * wide, wide)
            ref[kind, :, cols] = product(here, cols).astype(ref.dtype)

    def core_copy(kind, j):
        return copy(kind, j, core_send.at[kind, piece(j)], core_recv.at[kind, piece(j)], core_peer)

    def x_copy(j):
        return copy(2, j, x_send.at[piece(j)], x_recv.at[piece(j)], x_peer)

    def low_copy(kind, j, c, xx, device):
        return copy(kind, j, low_send.at[piece(j)], out.at[place_of(c, xx, j)], device)

    def relay(j, c, xx):
        return copy(5, j, out.at[place_of(c, xx, j)], out.at[place_of(c, xx, j)], core_peer)

    def keep(j):
        return pltpu.make_async_copy(low_send.at[piece(j)], out.at[place_of(core, x, j)], keep_sem.at[j])

    term(1 - core, 1 - x, core_send, 0)
    for j in range(PIECES):
        core_copy(0, j).start()
    term(core, 1 - x, part, 0)
    for j in range(PIECES):
        core_copy(0, j).wait_recv()
        x_send[piece(j), :] = (part[0, piece(j), :] + core_recv[0, piece(j), :].astype(F32)).astype(BF16)
        x_copy(j).start()
    term(1 - core, x, core_send, 1)
    for j in range(PIECES):
        core_copy(1, j).start()
    term(core, x, part, 1)
    fill_one()
    for j in range(PIECES):
        core_copy(1, j).wait_recv()
        x_copy(j).wait_recv()
        here = piece(j)
        total = part[1, here, :] + core_recv[1, here, :].astype(F32) + x_recv[here, :].astype(F32)
        low_send[here, :] = finish(here, total)
        low_copy(3, j, core, x, x_peer).start()
        low_copy(4, j, core, x, core_peer).start()
        keep(j).start()
    fill_two()
    for j in range(PIECES):
        low_copy(3, j, core, 1 - x, x_peer).wait_recv()
        relay(j, core, 1 - x).start()
    for j in range(PIECES):
        low_copy(4, j, 1 - core, x, core_peer).wait_recv()
        relay(j, 1 - core, 1 - x).wait_recv()
        keep(j).wait()
        core_copy(0, j).wait_send()
        core_copy(1, j).wait_send()
        x_copy(j).wait_send()
        low_copy(3, j, core, x, x_peer).wait_send()
        low_copy(4, j, core, x, core_peer).wait_send()
        relay(j, core, 1 - x).wait_send()


def exchange_scratch(block, features):
    return [
        pltpu.VMEM((2, block, features), BF16),
        pltpu.VMEM((2, block, features), BF16),
        pltpu.VMEM((2, block, features), F32),
        pltpu.VMEM((block, features), BF16),
        pltpu.VMEM((block, features), BF16),
        pltpu.VMEM((block, features), BF16),
        pltpu.SemaphoreType.DMA((6, PIECES)),
        pltpu.SemaphoreType.DMA((6, PIECES)),
        pltpu.SemaphoreType.DMA((PIECES,)),
    ]


def project_kernel(mixed_ref, weight_ref, own_ref, gain_ref, two_out, resid_out, *scratch):
    def product(rows, cols):
        return jnp.dot(mixed_ref[rows, :], weight_ref[:, cols], preferred_element_type=F32)

    def finish(rows, total):
        resid = own_ref[rows, :].astype(F32) + total
        resid_out[rows, :] = resid
        return (resid * rsqrt_mean(resid) * gain_ref[...]).astype(BF16)

    def nothing():
        return None

    exchange(mixed_ref.shape[0], weight_ref.shape[1], product, finish, nothing, nothing, two_out, scratch)


def project(mixed_low, out_weight, own, gain):
    tokens = mixed_low.shape[0]
    features = out_weight.shape[1]
    block = tokens // 4
    return pl.pallas_call(
        project_kernel,
        in_specs=[pl.BlockSpec(memory_space=pltpu.VMEM)] * 4,
        out_specs=[pl.BlockSpec(memory_space=pl.ANY), pl.BlockSpec(memory_space=pltpu.VMEM)],
        out_shape=[
            jax.ShapeDtypeStruct((tokens, features), BF16),
            jax.ShapeDtypeStruct((block, features), F32),
        ],
        scratch_shapes=exchange_scratch(block, features),
        compiler_params=params(22, collective_id=1, has_side_effects=True),
        cost_estimate=pl.CostEstimate(flops=2 * mixed_low.size * features, bytes_accessed=tokens * features * 80, transcendentals=0),
        name="project",
    )(mixed_low, out_weight, own, gain)


def pull_kernel(
    gate_ref, up_ref, gate_w, up_w, two_ref, resid_ref, cot_ref, gain_ref,
    low_out, gain_out, gate_grad, up_grad, *scratch,
):
    features = gate_w.shape[0]
    step = 256
    gain_out[...] = jnp.zeros_like(gain_out)

    def product(rows, cols):
        return lax.dot_general(
            gate_ref[rows, :], gate_w[cols, :], (((1,), (1,)), ((), ())), preferred_element_type=F32
        ) + lax.dot_general(up_ref[rows, :], up_w[cols, :], (((1,), (1,)), ((), ())), preferred_element_type=F32)

    def finish(rows, total):
        resid = resid_ref[rows, :]
        q = rsqrt_mean(resid)
        gain_out[...] += column_total(total * resid * q)
        weighed = gain_ref[...] * total
        pulled = q * weighed - resid * q * q * q * jnp.mean(weighed * resid, axis=-1, keepdims=True)
        return (cot_ref[rows, :].astype(F32) + pulled).astype(BF16)

    def weight_grad(source, target):
        def run(n, carry):
            cols = pl.ds(pl.multiple_of(n * step, step), step)
            target[cols, :] = lax.dot_general(
                two_ref[:, cols], source[...], (((0,), (0,)), ((), ())), preferred_element_type=F32
            ).astype(BF16)
            return carry

        def go():
            lax.fori_loop(0, features // step, run, 0)

        return go

    exchange(
        gate_ref.shape[0], features, product, finish,
        weight_grad(gate_ref, gate_grad), weight_grad(up_ref, up_grad), low_out, scratch,
    )


def pull(d_gate, d_up, gate_w, up_w, two_low, resid, cot, gain):
    tokens, hidden = d_gate.shape
    features = gate_w.shape[0]
    block = tokens // 4
    vmem = pl.BlockSpec(memory_space=pltpu.VMEM)
    return pl.pallas_call(
        pull_kernel,
        in_specs=[vmem] * 8,
        out_specs=[pl.BlockSpec(memory_space=pl.ANY), vmem, vmem, vmem],
        out_shape=[
            jax.ShapeDtypeStruct((tokens, features), BF16),
            jax.ShapeDtypeStruct((1, features), F32),
            jax.ShapeDtypeStruct((features, hidden), BF16),
            jax.ShapeDtypeStruct((features, hidden), BF16),
        ],
        scratch_shapes=exchange_scratch(block, features),
        compiler_params=params(46, collective_id=2, has_side_effects=True),
        cost_estimate=pl.CostEstimate(flops=8 * d_gate.size * features, bytes_accessed=tokens * features * 80, transcendentals=0),
        name="pull",
    )(d_gate, d_up, gate_w, up_w, two_low, resid, cot, gain)


def rsqrt_mean(v):
    return lax.rsqrt(jnp.mean(v * v, axis=-1, keepdims=True) + EPSILON)


def dot(a, b, left, right):
    return lax.dot_general(a, b, (((left,), (right,)), ((), ())), preferred_element_type=F32)


def body(
    n_dp,
    inputs,
    segment_ids,
    cotangent,
    first_gain,
    gate_weight,
    gate_bias,
    branch_weight,
    branch_bias,
    conv_weight,
    conv_bias,
    rate_weight,
    rate_bias,
    input_weight,
    input_bias,
    decay_param,
    out_weight,
    second_gain,
    ffn_gate,
    ffn_up,
    ffn_down,
):
    tokens, share = inputs.shape
    features = share * 4
    channels = gate_weight.shape[1]
    gain_one = first_gain.astype(F32)
    gain_two = second_gain.astype(F32)
    at = lax.axis_index("tensor")
    start = token_start(tokens)
    block = tokens // 4

    row = jnp.arange(tokens, dtype=jnp.int32)
    masks = []
    for k in range(4):
        offset = max(k, 1)
        earlier = jnp.concatenate([jnp.full((offset,), -1, jnp.int32), segment_ids[:-offset]])
        same = (row >= offset) & (segment_ids == earlier)
        masks.append(same if k else ~same)
    masks = jnp.pad(jnp.stack(masks, axis=1).astype(F32), ((0, HALO), (0, 0)))
    rows = jnp.concatenate(
        [
            conv_weight.astype(F32),
            jnp.concatenate([conv_bias, rate_bias, input_bias]).astype(F32).reshape(3, channels),
            jax.nn.softplus(-decay_param)[None],
        ]
    )

    across, masks, rows, gate_bias, branch_bias, gain_one, gain_two = lax.optimization_barrier(
        (swap_x(inputs), masks, rows, gate_bias.astype(F32), branch_bias.astype(F32), gain_one, gain_two)
    )
    in_pieces = (inputs, swap_core(inputs), across, swap_core(across))
    later_cot, _ = lax.optimization_barrier((cotangent, across))
    cot_across = swap_x(later_cot)
    whole_in = join_features(in_pieces)
    in_f = whole_in.astype(F32)
    q_one = rsqrt_mean(in_f)
    normed_low = lax.optimization_barrier((in_f * q_one * gain_one).astype(BF16))
    gate_pre = dot(normed_low, gate_weight, 1, 0) + gate_bias.astype(F32)
    branch_pre = dot(normed_low, branch_weight, 1, 0) + branch_bias.astype(F32)
    conv, rate, opened, state, mixed_low = forward_block(
        gate_pre, branch_pre, masks, rows, rate_weight, input_weight
    )
    mixed_low, cot_across = lax.optimization_barrier((mixed_low, cot_across))
    whole_cot = join_features((cotangent, swap_core(cotangent), cot_across, swap_core(cot_across)))
    two_low, resid = project(
        mixed_low, out_weight, lax.dynamic_slice_in_dim(whole_in, start, block, 0), gain_two[None]
    )
    d_hidden = dot(whole_cot, ffn_down, 1, 1)
    hidden_gate = dot(two_low, ffn_gate, 1, 0)
    hidden_up = dot(two_low, ffn_up, 1, 0)
    hidden_act, hidden_slope = gelu_parts(hidden_gate)
    hidden_low = (hidden_act * hidden_up).astype(BF16)
    cut = hidden_low.shape[1] * 4 // 9
    down_early = dot(hidden_low[:, :cut], whole_cot, 0, 0)
    down_late = dot(hidden_low[:, cut:], whole_cot, 0, 0)
    d_hgate = (d_hidden * hidden_up * hidden_slope).astype(BF16)
    d_hup = (d_hidden * hidden_act).astype(BF16)
    if n_dp == 8:
        down_early, down_late, d_hgate, d_hup = lax.optimization_barrier(
            (down_early.astype(BF16), down_late.astype(BF16), d_hgate, d_hup)
        )
        down_early = lax.psum(down_early, "dp")
    cot_mine = lax.dynamic_slice_in_dim(whole_cot, start, block, 0)
    d_resid_low, second_gain_grad, ffn_gate_grad, ffn_up_grad = pull(
        d_hgate, d_hup, ffn_gate, ffn_up, two_low, resid, cot_mine, gain_two[None]
    )
    second_gain_grad = second_gain_grad[0]
    d_mixed = dot(d_resid_low, out_weight, 1, 1)
    d_gate_low, d_branch_low, misc = backward_block(
        d_mixed, gate_pre, branch_pre, conv, rate, opened, state, masks, rows, rate_weight, input_weight
    )
    if n_dp == 8:
        down_early, down_late, d_gate_low = lax.optimization_barrier((down_early, down_late, d_gate_low))
        down_late = lax.psum(down_late, "dp")
    first_share = dot(d_gate_low, gate_weight, 1, 1) + dot(d_branch_low, branch_weight, 1, 1)
    product = first_share * in_f
    sums = jnp.concatenate([
        jnp.sum(product * q_one, axis=0), second_gain_grad, jnp.sum(product * gain_one, axis=1)
    ])
    sums = tensor_sum(sums.reshape(-1, LANES)).reshape(-1)
    gains = sums[: 2 * features].reshape(-1, channels)
    mean_one = sums[2 * features :, None] / features
    misc = lax.dynamic_update_slice_in_dim(misc, gains.astype(BF16), 2 * LANES + 16, 0)
    if n_dp == 8:
        (ffn_gate_grad, ffn_up_grad, misc, *summed), output, d_first = ring_all(
            [ffn_gate_grad, ffn_up_grad, misc],
            normed_low, d_gate_low, d_branch_low, mixed_low, d_resid_low, hidden_low, ffn_down, resid, first_share,
        )
        summed = [ffn_gate_grad, ffn_up_grad, *summed, misc]
        (*summed, down_late) = lax.optimization_barrier((*summed, down_late))
        summed = [a.astype(F32) for a in (jnp.concatenate([down_early, down_late]), *summed)]
    else:
        gate_weight_grad = dot(normed_low, d_gate_low, 0, 0)
        branch_weight_grad = dot(normed_low, d_branch_low, 0, 0)
        out_weight_grad = dot(mixed_low, d_resid_low, 0, 0)
        summed = [ffn_gate_grad, ffn_up_grad, gate_weight_grad, branch_weight_grad, out_weight_grad, misc]
        summed = dp_sum([jnp.concatenate([down_early, down_late]), *summed], n_dp)
        first_here, first_there = scatter_features(first_share)
        d_first = first_here + first_there.astype(F32)
        ffn_part = dot(hidden_low, ffn_down, 1, 0)
        with_resid = lax.dynamic_slice_in_dim(ffn_part, start, block, 0) + resid
        ffn_part = lax.dynamic_update_slice_in_dim(ffn_part, with_resid, start, 0)
        output_here, output_there = scatter_features(ffn_part)
        output = (output_here + output_there.astype(F32)).astype(BF16)
    ffn_down_grad, ffn_gate_grad, ffn_up_grad, gate_weight_grad, branch_weight_grad, out_weight_grad, misc = summed

    own_in = inputs.astype(F32)
    own_gain = lax.dynamic_slice_in_dim(gain_one, at * share, share, 0)
    input_grad = (
        lax.dynamic_slice_in_dim(d_resid_low, at * share, share, 1).astype(F32)
        + q_one * own_gain * d_first
        - own_in * q_one * q_one * q_one * mean_one
    )
    heads = rate_weight.shape[0]

    def blocks(v):
        return v.reshape(LANES, heads, LANES).transpose(1, 0, 2)

    small = misc[2 * LANES : 2 * LANES + 16]
    gains = misc[2 * LANES + 16 : 2 * LANES + 16 + gains.shape[0]].reshape(2, features)
    decay_grad = -small[7] * jax.nn.sigmoid(-decay_param)
    return (
        output,
        input_grad,
        gains[0],
        gate_weight_grad,
        small[8],
        branch_weight_grad,
        small[9],
        small[0:4],
        small[4],
        blocks(misc[:LANES]),
        small[5],
        blocks(misc[LANES : 2 * LANES]),
        small[6],
        decay_grad,
        out_weight_grad,
        gains[1],
        ffn_gate_grad,
        ffn_up_grad,
        ffn_down_grad,
    )


def solution(mesh):
    in_specs = (
        P("dp", "tensor"),
        P("dp"),
        P("dp", "tensor"),
        P(),
        P(None, "tensor"),
        P("tensor"),
        P(None, "tensor"),
        P("tensor"),
        P(None, "tensor"),
        P("tensor"),
        P("tensor", None, None),
        P("tensor"),
        P("tensor", None, None),
        P("tensor"),
        P("tensor"),
        P("tensor", None),
        P(),
        P(None, "tensor"),
        P(None, "tensor"),
        P("tensor", None),
    )
    out_specs = (
        P("dp", "tensor"),
        P("dp", "tensor"),
        P(),
        P(None, "tensor"),
        P("tensor"),
        P(None, "tensor"),
        P("tensor"),
        P(None, "tensor"),
        P("tensor"),
        P("tensor", None, None),
        P("tensor"),
        P("tensor", None, None),
        P("tensor"),
        P("tensor"),
        P("tensor", None),
        P(),
        P(None, "tensor"),
        P(None, "tensor"),
        P("tensor", None),
    )
    return jax.shard_map(
        functools.partial(body, mesh.shape["dp"]), mesh=mesh, in_specs=in_specs, out_specs=out_specs, check_vma=False
    )
```

```python
import functools

import jax
import jax.numpy as jnp
from jax import lax
from jax.experimental import pallas as pl
from jax.experimental.pallas import tpu as pltpu
from jax.sharding import PartitionSpec as P

EPSILON = 1e-06
FLOOR = 0.05
F32 = jnp.float32
BF16 = jnp.bfloat16
LANES = 128
SPAN = 32
HALO = 8
MIB = 1024 * 1024


def params(mib, **more):
    return pltpu.CompilerParams(vmem_limit_bytes=mib * MIB, **more)


def gelu_parts(v):
    c0 = 0.7978845608028654
    c1 = 0.044715
    t = jnp.tanh(c0 * (v + c1 * v * v * v))
    act = 0.5 * v * (1.0 + t)
    slope = 0.5 * (1.0 + t) + 0.5 * v * (1.0 - t * t) * c0 * (1.0 + 3.0 * c1 * v * v)
    return act, slope


def sigmoid(v):
    return 0.5 * jnp.tanh(0.5 * v) + 0.5


def shift_down(v, amount, fill):
    row = lax.broadcasted_iota(jnp.int32, v.shape, 0)
    return jnp.where(row >= amount, pltpu.roll(v, amount, 0), fill)


def shift_up(v, amount, fill):
    row = lax.broadcasted_iota(jnp.int32, v.shape, 0)
    size = v.shape[0]
    return jnp.where(row < size - amount, pltpu.roll(v, size - amount, 0), fill)


def scale_of(decayed, reset):
    rest = 1.0 - decayed * decayed
    return jnp.where(reset, 1.0, jnp.sqrt(jnp.maximum(rest, FLOOR))), rest


def forward_kernel(
    gate_ref, branch_ref, mask_ref, row_ref, rate_w, input_w,
    conv_out, rate_out, open_out, state_out, mixed_out, padded, keep_s, local_s,
):
    tokens = gate_ref.shape[0]
    step = 128
    spans = tokens // SPAN
    padded[0:HALO, :] = jnp.zeros((HALO, LANES), F32)
    padded[HALO:, :] = branch_ref[...]
    wr = rate_w[0]
    wi = input_w[0]

    def fill(i, carry):
        r0 = pl.multiple_of(i * step, step)
        here = pl.ds(r0, step)
        wide = padded[pl.ds(r0, step + HALO), :]
        total = row_ref[4:5, :] + row_ref[0:1, :] * wide[HALO:, :]
        for k in range(1, 4):
            total = total + row_ref[k : k + 1, :] * wide[HALO - k : HALO - k + step, :] * mask_ref[here, k : k + 1]
        low = total.astype(BF16)
        rate = sigmoid(jnp.dot(low, wr, preferred_element_type=F32) + row_ref[5:6, :])
        opened = sigmoid(jnp.dot(low, wi, preferred_element_type=F32) + row_ref[6:7, :])
        reset = mask_ref[here, 0:1] > 0.5
        decayed = jnp.exp(-8.0 * rate * row_ref[7:8, :])
        scale, _ = scale_of(decayed, reset)
        conv_out[here, :] = total
        rate_out[here, :] = rate
        open_out[here, :] = opened
        keep_s[here, :] = jnp.where(reset, 0.0, decayed)
        state_out[here, :] = scale * opened * total
        return carry

    lax.fori_loop(0, tokens // step, fill, 0)
    h = jnp.zeros((spans, LANES), F32)
    p = jnp.ones((spans, LANES), F32)
    for k in range(SPAN):
        at = pl.ds(k, spans, stride=SPAN)
        a = keep_s[at, :]
        h = a * h + state_out[at, :]
        p = p * a
        local_s[at, :] = h
        keep_s[at, :] = p
    jump = 1
    while jump < spans:
        h = h + p * shift_down(h, jump, 0.0)
        p = p * shift_down(p, jump, 1.0)
        jump *= 2
    carry_in = shift_down(h, 1, 0.0)
    for k in range(SPAN):
        at = pl.ds(k, spans, stride=SPAN)
        state_out[at, :] = local_s[at, :] + keep_s[at, :] * carry_in

    def mix(i, carry):
        here = pl.ds(pl.multiple_of(i * step, step), step)
        act, _ = gelu_parts(gate_ref[here, :])
        mixed_out[here, :] = (act * state_out[here, :]).astype(BF16)
        return carry

    lax.fori_loop(0, tokens // step, mix, 0)


def forward_block(gate_pre, branch_pre, masks, rows, rate_weight, input_weight):
    tokens, channels = gate_pre.shape
    heads = rate_weight.shape[0]
    col = pl.BlockSpec((tokens, LANES), lambda h: (0, h))
    whole = pl.BlockSpec(masks.shape, lambda h: (0, 0))
    table = pl.BlockSpec((8, LANES), lambda h: (0, h))
    square = pl.BlockSpec((1, LANES, LANES), lambda h: (h, 0, 0))
    full = jax.ShapeDtypeStruct((tokens, channels), F32)
    return pl.pallas_call(
        forward_kernel,
        grid=(heads,),
        in_specs=[col, col, whole, table, square, square],
        out_specs=[col] * 5,
        out_shape=[full] * 4 + [jax.ShapeDtypeStruct((tokens, channels), BF16)],
        scratch_shapes=[
            pltpu.VMEM((tokens + HALO, LANES), F32),
            pltpu.VMEM((tokens, LANES), F32),
            pltpu.VMEM((tokens, LANES), F32),
        ],
        compiler_params=params(60),
        cost_estimate=pl.CostEstimate(flops=tokens * channels * 700, bytes_accessed=tokens * channels * 26, transcendentals=tokens * channels * 5),
        name="recurrence_forward",
    )(gate_pre, branch_pre, masks, rows, rate_weight, input_weight)


def column_total(v):
    return jnp.sum(v, axis=0, keepdims=True)


def backward_kernel(
    dmix_ref, gate_ref, branch_ref, conv_ref, rate_ref, open_ref, state_ref, mask_ref, row_ref, rate_w, input_w,
    dgate_out, dbranch_out, misc_out, padded, keep_s, adj_s, dconv_s, prev_s, rate_g, input_g, small_g,
):
    tokens = gate_ref.shape[0]
    step = 128
    count = tokens // step
    spans = tokens // SPAN
    zero_halo = jnp.zeros((HALO, LANES), F32)
    padded[0:HALO, :] = zero_halo
    padded[HALO:, :] = branch_ref[...]
    prev_s[0:HALO, :] = zero_halo
    prev_s[HALO:, :] = state_ref[...]
    keep_s[tokens:, :] = zero_halo
    dconv_s[tokens:, :] = zero_halo
    wr = rate_w[0]
    wi = input_w[0]

    def fill(i, total):
        here = pl.ds(pl.multiple_of(i * step, step), step)
        act, slope = gelu_parts(gate_ref[here, :])
        dmix = dmix_ref[here, :]
        dgate = (dmix * state_ref[here, :] * slope).astype(BF16)
        dgate_out[here, :] = dgate
        adj_s[here, :] = dmix * act
        reset = mask_ref[here, 0:1] > 0.5
        keep_s[here, :] = jnp.where(reset, 0.0, jnp.exp(-8.0 * rate_ref[here, :] * row_ref[7:8, :]))
        return total + column_total(dgate.astype(F32))

    gate_bias = lax.fori_loop(0, count, fill, jnp.zeros((1, LANES), F32))
    h = jnp.zeros((spans, LANES), F32)
    p = jnp.ones((spans, LANES), F32)
    for k in reversed(range(SPAN)):
        at = pl.ds(k, spans, stride=SPAN)
        a = keep_s[pl.ds(k + 1, spans, stride=SPAN), :]
        h = a * h + adj_s[at, :]
        p = p * a
        adj_s[at, :] = h
        dconv_s[at, :] = p
    jump = 1
    while jump < spans:
        h = h + p * shift_up(h, jump, 0.0)
        p = p * shift_up(p, jump, 1.0)
        jump *= 2
    carry_in = shift_up(h, 1, 0.0)
    for k in range(SPAN):
        at = pl.ds(k, spans, stride=SPAN)
        adj_s[at, :] = adj_s[at, :] + dconv_s[at, :] * carry_in

    nothing = jnp.zeros((1, LANES), F32)
    rate_g[...] = jnp.zeros_like(rate_g)
    input_g[...] = jnp.zeros_like(input_g)

    def gates(i, totals):
        r0 = pl.multiple_of(i * step, step)
        here = pl.ds(r0, step)
        adj = adj_s[here, :]
        conv = conv_ref[here, :]
        rate = rate_ref[here, :]
        opened = open_ref[here, :]
        reset = mask_ref[here, 0:1] > 0.5
        decay_row = row_ref[7:8, :]
        decayed = jnp.exp(-8.0 * rate * decay_row)
        scale, rest = scale_of(decayed, reset)
        before = prev_s[pl.ds(r0, step + HALO), :][HALO - 1 : HALO - 1 + step, :]
        pull = jnp.where(rest > FLOOR, 1.0, jnp.where(rest == FLOOR, 0.5, 0.0))
        d_scale = adj * opened * conv
        d_decayed = jnp.where(reset, 0.0, adj * before - d_scale * pull * decayed / scale)
        d_log = d_decayed * decayed * -8.0
        d_rate = (d_log * decay_row * rate * (1.0 - rate)).astype(BF16)
        d_input = (adj * scale * conv * opened * (1.0 - opened)).astype(BF16)
        d_conv = (
            adj * scale * opened
            + lax.dot_general(d_rate, wr, (((1,), (1,)), ((), ())), preferred_element_type=F32)
            + lax.dot_general(d_input, wi, (((1,), (1,)), ((), ())), preferred_element_type=F32)
        )
        dconv_s[here, :] = d_conv
        low = conv.astype(BF16)
        rate_g[...] += lax.dot_general(low, d_rate, (((0,), (0,)), ((), ())), preferred_element_type=F32)
        input_g[...] += lax.dot_general(low, d_input, (((0,), (0,)), ((), ())), preferred_element_type=F32)
        wide = padded[pl.ds(r0, step + HALO), :]
        news = [
            column_total(d_conv * wide[HALO:, :]),
            *[
                column_total(d_conv * mask_ref[here, k : k + 1] * wide[HALO - k : HALO - k + step, :])
                for k in range(1, 4)
            ],
            column_total(d_conv),
            column_total(d_rate.astype(F32)),
            column_total(d_input.astype(F32)),
            column_total(d_log * rate),
        ]
        return tuple(t + n for t, n in zip(totals, news))

    totals = lax.fori_loop(0, count, gates, (nothing,) * 8)

    def conv_back(i, total):
        r0 = pl.multiple_of(i * step, step)
        here = pl.ds(r0, step)
        wide = dconv_s[pl.ds(r0, step + HALO), :]
        d_branch = row_ref[0:1, :] * wide[:step, :]
        for k in range(1, 4):
            part = wide * mask_ref[pl.ds(r0, step + HALO), k : k + 1]
            d_branch = d_branch + row_ref[k : k + 1, :] * part[k : k + step, :]
        low = d_branch.astype(BF16)
        dbranch_out[here, :] = low
        return total + column_total(low.astype(F32))

    branch_bias = lax.fori_loop(0, count, conv_back, nothing)
    small_g[...] = jnp.zeros_like(small_g)
    for at, value in enumerate((*totals, gate_bias, branch_bias)):
        small_g[at : at + 1, :] = value
    misc_out[...] = jnp.zeros_like(misc_out)
    misc_out[0:LANES, :] = rate_g[...].astype(BF16)
    misc_out[LANES : 2 * LANES, :] = input_g[...].astype(BF16)
    misc_out[2 * LANES : 2 * LANES + 16, :] = small_g[...].astype(BF16)


def backward_block(d_mixed, gate_pre, branch_pre, conv, rate, opened, state, masks, rows, rate_weight, input_weight):
    tokens, channels = gate_pre.shape
    heads = rate_weight.shape[0]
    col = pl.BlockSpec((tokens, LANES), lambda h: (0, h))
    whole = pl.BlockSpec(masks.shape, lambda h: (0, 0))
    table = pl.BlockSpec((8, LANES), lambda h: (0, h))
    square = pl.BlockSpec((1, LANES, LANES), lambda h: (h, 0, 0))
    misc = pl.BlockSpec((3 * LANES, LANES), lambda h: (0, h))
    return pl.pallas_call(
        backward_kernel,
        grid=(heads,),
        in_specs=[col] * 7 + [whole, table, square, square],
        out_specs=[col, col, misc],
        out_shape=[
            jax.ShapeDtypeStruct((tokens, channels), BF16),
            jax.ShapeDtypeStruct((tokens, channels), BF16),
            jax.ShapeDtypeStruct((3 * LANES, channels), BF16),
        ],
        scratch_shapes=[
            pltpu.VMEM((tokens + HALO, LANES), F32),
            pltpu.VMEM((tokens + HALO, LANES), F32),
            pltpu.VMEM((tokens, LANES), F32),
            pltpu.VMEM((tokens + HALO, LANES), F32),
            pltpu.VMEM((tokens + HALO, LANES), F32),
            pltpu.VMEM((LANES, LANES), F32),
            pltpu.VMEM((LANES, LANES), F32),
            pltpu.VMEM((16, LANES), F32),
        ],
        compiler_params=params(60),
        cost_estimate=pl.CostEstimate(flops=tokens * channels * 1400, bytes_accessed=tokens * channels * 32, transcendentals=tokens * channels * 5),
        name="recurrence_backward",
    )(d_mixed, gate_pre, branch_pre, conv, rate, opened, state, masks, rows, rate_weight, input_weight)


X_PAIRS = [(0, 2), (2, 0), (1, 3), (3, 1)]
CORE_PAIRS = [(0, 1), (1, 0), (2, 3), (3, 2)]


def swap_x(v):
    return lax.ppermute(v, "tensor", X_PAIRS)


def swap_core(v):
    return lax.ppermute(v, "tensor", CORE_PAIRS)


def place():
    at = lax.axis_index("tensor")
    return at // 2, at % 2


def share_features(v):
    across = swap_x(v)
    return v, swap_core(v), across, swap_core(across)


def join_features(pieces):
    at = lax.axis_index("tensor")
    rows, share = pieces[0].shape
    out = jnp.zeros((rows, share * 4), pieces[0].dtype)
    for distance, piece in enumerate(pieces):
        out = lax.dynamic_update_slice_in_dim(out, piece, (at ^ distance) * share, 1)
    return out


def token_start(tokens):
    x, core = place()
    return (core * 2 + x) * (tokens // 4)


def scatter_tokens(v):
    x, core = place()
    half = v.shape[0] // 2
    mine = lax.dynamic_slice_in_dim(v, core * half, half, 0)
    other = lax.dynamic_slice_in_dim(v, (1 - core) * half, half, 0)
    both = mine + swap_core(other.astype(BF16)).astype(F32)
    quarter = half // 2
    mine = lax.dynamic_slice_in_dim(both, x * quarter, quarter, 0)
    other = lax.dynamic_slice_in_dim(both, (1 - x) * quarter, quarter, 0)
    return mine + swap_x(other.astype(BF16)).astype(F32)


def gather_tokens(v):
    x, core = place()
    block = v.shape[0]
    across = swap_x(v)
    near = swap_core(v)
    far = swap_core(across)
    out = jnp.zeros((block * 4, v.shape[1]), v.dtype)
    for piece, where in (
        (v, core * 2 + x),
        (near, (1 - core) * 2 + x),
        (across, core * 2 + 1 - x),
        (far, (1 - core) * 2 + 1 - x),
    ):
        out = lax.dynamic_update_slice_in_dim(out, piece, where * block, 0)
    return out


def scatter_features(v):
    x, core = place()
    share = v.shape[1] // 4

    def part(at):
        return lax.dynamic_slice_in_dim(v, at * share, share, 1)

    def pair(c):
        return part(x * 2 + c), part((1 - x) * 2 + c)

    mine, other = pair(core)
    send_mine, send_other = pair(1 - core)
    got_mine = swap_core(send_mine.astype(BF16)).astype(F32)
    got_other = swap_core(send_other.astype(BF16)).astype(F32)
    return mine + got_mine, swap_x((other + got_other).astype(BF16))


def tensor_sum(v):
    v = v + swap_core(v)
    return v + swap_x(v)


MESH = pl.DeviceIdType.MESH
HELD = 9


def ring_kernel(given, n, *refs):
    count = given + 3
    ins, extra, refs = refs[:given], refs[given : given + HELD], refs[given + HELD :]
    outs, sums, refs = refs[:count], refs[count : count + 2], refs[count + 2 :]
    slots, locals_, refs = refs[:count], refs[count : 2 * count], refs[2 * count :]
    send_sem, recv_sem, load_sem, keep_sem = refs[:4]
    held, refs = refs[4 : 4 + HELD], refs[4 + HELD :]
    core_send, core_recv, x_send, x_recv, own, other, held_sem, share_send, share_recv = refs[:9]
    made = refs[9:]
    ins = (*ins, *made)
    normed_s, gate_s, branch_s, mixed_s, low_s, hidden_s, down_s, resid_s, first_s = held
    me = lax.axis_index("dp")
    y = lax.rem(me, 2)
    z = me // 2
    p = jnp.where(y == 0, z, n - 1 - z)

    def device(at):
        return jnp.where(at < n // 2, 2 * at, 2 * (n - 1 - at) + 1)

    after, before = device(lax.rem(p + 1, n)), device(lax.rem(p + n - 1, n))
    targets = (after, before)
    at = lax.axis_index("tensor")
    core = lax.rem(at, 2)
    x = at // 2
    core_peer = x * 2 + 1 - core
    x_peer = (1 - x) * 2 + core
    barrier = pltpu.get_barrier_semaphore()
    for target in targets:
        pl.semaphore_signal(barrier, inc=1, device_id={"dp": target}, device_id_type=MESH)
    for target in (core_peer, x_peer):
        pl.semaphore_signal(barrier, inc=1, device_id={"tensor": target}, device_id_type=MESH)
    pl.semaphore_wait(barrier, 4)

    def hold(i):
        return pltpu.make_async_copy(extra[i], held[i], held_sem.at[i])

    tokens, share = own.shape
    block = tokens // 4

    def share_copy(kind, i):
        if i < 2:
            source, target, device = core_send.at[kind, i], core_recv.at[kind, i], core_peer
        else:
            source, target, device = x_send.at[kind], x_recv.at[kind], x_peer
        return pltpu.make_async_remote_copy(
            source, target, share_send.at[kind, i], share_recv.at[kind, i],
            device_id={"tensor": device}, device_id_type=MESH,
        )

    def share_cols(xx, c):
        return pl.ds(pl.multiple_of((xx * 2 + c) * share, LANES), share)

    def output_terms(b):
        rows = pl.ds(b * block, block)
        mine = jnp.where(core * 2 + x == b, 1.0, 0.0)
        for xx, c, ref in (
            (1 - x, 1 - core, core_send.at[0, 1]),
            (x, 1 - core, core_send.at[0, 0]),
            (1 - x, core, other),
            (x, core, own),
        ):
            cols = share_cols(xx, c)
            term = jnp.dot(hidden_s[rows, :], down_s[:, cols], preferred_element_type=F32) + mine * resid_s[:, cols]
            ref[rows, :] = term.astype(ref.dtype)

    def first_terms():
        core_send[1, 1] = first_s[:, share_cols(1 - x, 1 - core)].astype(BF16)
        core_send[1, 0] = first_s[:, share_cols(x, 1 - core)].astype(BF16)

    def share_start(kind):
        share_copy(kind, 1).start()
        share_copy(kind, 0).start()

    def share_forward(kind):
        share_copy(kind, 1).wait_recv()
        far = first_s[:, share_cols(1 - x, core)] if kind else other[...]
        x_send[kind] = (far + core_recv[kind, 1].astype(F32)).astype(BF16)
        share_copy(kind, 2).start()

    def share_finish(kind):
        share_copy(kind, 0).wait_recv()
        share_copy(kind, 2).wait_recv()
        near = first_s[:, share_cols(x, core)] if kind else own[...]
        total = near + core_recv[kind, 0].astype(F32) + x_recv[kind].astype(F32)
        sums[kind][...] = total.astype(sums[kind].dtype)

    def weight_grad(source, by, target):
        def run(i, carry):
            cols = pl.ds(pl.multiple_of(i * 256, 256), 256)
            target[cols, :] = lax.dot_general(
                source[:, cols], by[...], (((0,), (0,)), ((), ())), preferred_element_type=F32
            ).astype(BF16)
            return carry

        lax.fori_loop(0, source.shape[1] // 256, run, 0)

    def piece(ref, q, side, chunk):
        rows = ref.shape[0] // (2 * n)
        start = pl.multiple_of((2 * lax.rem(chunk + n, n) + side) * rows, 8)
        return ref.at[pl.ds(start, rows), :]

    def arriving(side, s):
        if s < n - 1:
            return p - 1 - s if side == 0 else p + 1 + s
        s -= n - 1
        return p - s if side == 0 else p + s

    def send(q, side, s, source):
        if s < n - 1:
            target = slots[q].at[s, side]
        else:
            chunk = p + 1 - (s - n + 1) if side == 0 else p - 1 + (s - n + 1)
            target = piece(outs[q], q, side, chunk + n)
        copy = pltpu.make_async_remote_copy(
            source, target, send_sem.at[q, side, s], recv_sem.at[q, side, s],
            device_id={"dp": targets[side]}, device_id_type=MESH,
        )
        copy.start()

    def wait(q, side, s, which):
        if s < n - 1:
            shape = slots[q].at[s, side]
        else:
            shape = piece(outs[q], q, side, arriving(side, s) + n)
        copy = pltpu.make_async_remote_copy(
            shape, shape, send_sem.at[q, side, s], recv_sem.at[q, side, s],
            device_id={"dp": targets[side]}, device_id_type=MESH,
        )
        (copy.wait_recv if which else copy.wait_send)()

    def load(q, side, s):
        return pltpu.make_async_copy(
            piece(ins[q], q, side, arriving(side, s) + n), locals_[q].at[s % 2, side], load_sem.at[q, side, s % 2]
        )

    def begin(q):
        for side in range(2):
            send(q, side, 0, piece(ins[q], q, side, p + n))
            load(q, side, 0).start()

    for q in range(given):
        begin(q)
    for i in range(HELD):
        hold(i).start()
    for i in range(5):
        hold(i).wait()
    for i, (source, by) in enumerate(((normed_s, gate_s), (normed_s, branch_s), (mixed_s, low_s))):
        weight_grad(source, by, made[i])
        begin(given + i)
    for i in range(5, HELD):
        hold(i).wait()
    for s in range(n - 1):
        if s == 1:
            share_start(0)
            first_terms()
            share_start(1)
        if s == 2:
            share_forward(0)
        if s == 3:
            share_forward(1)
        if s == 5:
            share_finish(0)
        if s == 6:
            share_finish(1)
        for q in range(count):
            if s == 0 and q < 4:
                output_terms(q)
            for side in range(2):
                if s + 1 < n - 1:
                    load(q, side, s + 1).start()
                load(q, side, s).wait()
                wait(q, side, s, True)
                slot = slots[q].at[s, side]
                slot[...] = (slot[...].astype(F32) + locals_[q][s % 2, side].astype(F32)).astype(BF16)
                send(q, side, s + 1, slot)
                if s == n - 2:
                    chunk = p + 1 if side == 0 else p - 1
                    pltpu.make_async_copy(slot, piece(outs[q], q, side, chunk + n), keep_sem.at[q, side]).start()
    for s in range(n - 1, 2 * n - 2):
        for q in range(count):
            for side in range(2):
                wait(q, side, s, True)
                if s + 1 < 2 * n - 2:
                    send(q, side, s + 1, piece(outs[q], q, side, arriving(side, s) + n))
    for q in range(count):
        for side in range(2):
            slot = slots[q].at[n - 2, side]
            chunk = p + 1 if side == 0 else p - 1
            pltpu.make_async_copy(slot, piece(outs[q], q, side, chunk + n), keep_sem.at[q, side]).wait()
            for s in range(2 * n - 2):
                wait(q, side, s, False)
    for kind in range(2):
        for i in range(3):
            share_copy(kind, i).wait_send()


def ring_all(arrays, normed, d_gate, d_branch, mixed, low, hidden, down, resid, first):
    n = 8
    given = len(arrays)
    made = [
        jax.ShapeDtypeStruct((a.shape[1], b.shape[1]), BF16)
        for a, b in ((normed, d_gate), (normed, d_branch), (mixed, low))
    ]
    reduced = [*arrays, *made]
    count = len(reduced)
    halves = [(a.shape[0] // (2 * n), a.shape[1]) for a in reduced]
    size = sum(a.size for a in reduced)
    extra = (normed, d_gate, d_branch, mixed, low, hidden, down, resid, first)
    tokens = hidden.shape[0]
    share = down.shape[1] // 4
    hbm = pl.BlockSpec(memory_space=pl.ANY)
    out = pl.pallas_call(
        functools.partial(ring_kernel, given, n),
        in_specs=[hbm] * (given + HELD),
        out_specs=[hbm] * count + [pl.BlockSpec(memory_space=pltpu.VMEM)] * 2,
        out_shape=[
            *[jax.ShapeDtypeStruct(a.shape, BF16) for a in reduced],
            jax.ShapeDtypeStruct((tokens, share), BF16),
            jax.ShapeDtypeStruct((tokens, share), F32),
        ],
        scratch_shapes=[
            *[pltpu.VMEM((n - 1, 2, *h), BF16) for h in halves],
            *[pltpu.VMEM((2, 2, *h), BF16) for h in halves],
            pltpu.SemaphoreType.DMA((count, 2, 2 * n - 2)),
            pltpu.SemaphoreType.DMA((count, 2, 2 * n - 2)),
            pltpu.SemaphoreType.DMA((count, 2, 2)),
            pltpu.SemaphoreType.DMA((count, 2)),
            *[pltpu.VMEM(a.shape, a.dtype) for a in extra],
            pltpu.VMEM((2, 2, tokens, share), BF16),
            pltpu.VMEM((2, 2, tokens, share), BF16),
            pltpu.VMEM((2, tokens, share), BF16),
            pltpu.VMEM((2, tokens, share), BF16),
            pltpu.VMEM((tokens, share), F32),
            pltpu.VMEM((tokens, share), F32),
            pltpu.SemaphoreType.DMA((HELD,)),
            pltpu.SemaphoreType.DMA((2, 3)),
            pltpu.SemaphoreType.DMA((2, 3)),
            *[pltpu.VMEM(a.shape, BF16) for a in made],
        ],
        compiler_params=params(63, collective_id=0, has_side_effects=True),
        cost_estimate=pl.CostEstimate(flops=2 * size, bytes_accessed=100 * size, transcendentals=0),
        name="ring_all",
    )(*arrays, *extra)
    return out[:count], out[count], out[count + 1]


def dp_sum(arrays, n):
    return [
        lax.all_gather(
            lax.psum_scatter(a, "dp", scatter_dimension=0, tiled=True).astype(BF16), "dp", axis=0, tiled=True
        ).astype(F32)
        if a.shape[0] % n == 0
        else lax.psum(a, "dp")
        for a in arrays
    ]


PIECES = 4


def exchange(tokens, features, product, finish, fill_one, fill_two, out, scratch):
    core_send, core_recv, part, x_send, x_recv, low_send, send_sem, recv_sem, keep_sem = scratch
    at = lax.axis_index("tensor")
    core = lax.rem(at, 2)
    x = at // 2
    core_peer = x * 2 + 1 - core
    x_peer = (1 - x) * 2 + core
    block = tokens // 4
    rows = block // PIECES
    wide = features // 3
    barrier = pltpu.get_barrier_semaphore()
    for target in (core_peer, x_peer):
        pl.semaphore_signal(barrier, inc=1, device_id={"tensor": target}, device_id_type=MESH)
    pl.semaphore_wait(barrier, 2)

    def copy(kind, j, source, target, device):
        return pltpu.make_async_remote_copy(
            source, target, send_sem.at[kind, j], recv_sem.at[kind, j],
            device_id={"tensor": device}, device_id_type=MESH,
        )

    def place_of(c, xx, j):
        return pl.ds(pl.multiple_of((c * 2 + xx) * block + j * rows, rows), rows)

    def piece(j):
        return pl.ds(j * rows, rows)

    def term(c, xx, ref, kind):
        here = pl.ds(pl.multiple_of((c * 2 + xx) * block, block), block)
        for n in range(3):
            cols = pl.ds(n * wide, wide)
            ref[kind, :, cols] = product(here, cols).astype(ref.dtype)

    def core_copy(kind, j):
        return copy(kind, j, core_send.at[kind, piece(j)], core_recv.at[kind, piece(j)], core_peer)

    def x_copy(j):
        return copy(2, j, x_send.at[piece(j)], x_recv.at[piece(j)], x_peer)

    def low_copy(kind, j, c, xx, device):
        return copy(kind, j, low_send.at[piece(j)], out.at[place_of(c, xx, j)], device)

    def relay(j, c, xx):
        return copy(5, j, out.at[place_of(c, xx, j)], out.at[place_of(c, xx, j)], core_peer)

    def keep(j):
        return pltpu.make_async_copy(low_send.at[piece(j)], out.at[place_of(core, x, j)], keep_sem.at[j])

    term(1 - core, 1 - x, core_send, 0)
    for j in range(PIECES):
        core_copy(0, j).start()
    term(core, 1 - x, part, 0)
    for j in range(PIECES):
        core_copy(0, j).wait_recv()
        x_send[piece(j), :] = (part[0, piece(j), :] + core_recv[0, piece(j), :].astype(F32)).astype(BF16)
        x_copy(j).start()
    term(1 - core, x, core_send, 1)
    for j in range(PIECES):
        core_copy(1, j).start()
    term(core, x, part, 1)
    fill_one()
    for j in range(PIECES):
        core_copy(1, j).wait_recv()
        x_copy(j).wait_recv()
        here = piece(j)
        total = part[1, here, :] + core_recv[1, here, :].astype(F32) + x_recv[here, :].astype(F32)
        low_send[here, :] = finish(here, total)
        low_copy(3, j, core, x, x_peer).start()
        low_copy(4, j, core, x, core_peer).start()
        keep(j).start()
    fill_two()
    for j in range(PIECES):
        low_copy(3, j, core, 1 - x, x_peer).wait_recv()
        relay(j, core, 1 - x).start()
    for j in range(PIECES):
        low_copy(4, j, 1 - core, x, core_peer).wait_recv()
        relay(j, 1 - core, 1 - x).wait_recv()
        keep(j).wait()
        core_copy(0, j).wait_send()
        core_copy(1, j).wait_send()
        x_copy(j).wait_send()
        low_copy(3, j, core, x, x_peer).wait_send()
        low_copy(4, j, core, x, core_peer).wait_send()
        relay(j, core, 1 - x).wait_send()


def exchange_scratch(block, features):
    return [
        pltpu.VMEM((2, block, features), BF16),
        pltpu.VMEM((2, block, features), BF16),
        pltpu.VMEM((2, block, features), F32),
        pltpu.VMEM((block, features), BF16),
        pltpu.VMEM((block, features), BF16),
        pltpu.VMEM((block, features), BF16),
        pltpu.SemaphoreType.DMA((6, PIECES)),
        pltpu.SemaphoreType.DMA((6, PIECES)),
        pltpu.SemaphoreType.DMA((PIECES,)),
    ]


def project_kernel(mixed_ref, weight_ref, own_ref, gain_ref, two_out, resid_out, *scratch):
    def product(rows, cols):
        return jnp.dot(mixed_ref[rows, :], weight_ref[:, cols], preferred_element_type=F32)

    def finish(rows, total):
        resid = own_ref[rows, :].astype(F32) + total
        resid_out[rows, :] = resid
        return (resid * rsqrt_mean(resid) * gain_ref[...]).astype(BF16)

    def nothing():
        return None

    exchange(mixed_ref.shape[0], weight_ref.shape[1], product, finish, nothing, nothing, two_out, scratch)


def project(mixed_low, out_weight, own, gain):
    tokens = mixed_low.shape[0]
    features = out_weight.shape[1]
    block = tokens // 4
    return pl.pallas_call(
        project_kernel,
        in_specs=[pl.BlockSpec(memory_space=pltpu.VMEM)] * 4,
        out_specs=[pl.BlockSpec(memory_space=pl.ANY), pl.BlockSpec(memory_space=pltpu.VMEM)],
        out_shape=[
            jax.ShapeDtypeStruct((tokens, features), BF16),
            jax.ShapeDtypeStruct((block, features), F32),
        ],
        scratch_shapes=exchange_scratch(block, features),
        compiler_params=params(22, collective_id=1, has_side_effects=True),
        cost_estimate=pl.CostEstimate(flops=2 * mixed_low.size * features, bytes_accessed=tokens * features * 80, transcendentals=0),
        name="project",
    )(mixed_low, out_weight, own, gain)


def pull_kernel(
    gate_ref, up_ref, gate_w, up_w, two_ref, resid_ref, cot_ref, gain_ref,
    low_out, gain_out, gate_grad, up_grad, *scratch,
):
    features = gate_w.shape[0]
    step = 256
    gain_out[...] = jnp.zeros_like(gain_out)

    def product(rows, cols):
        return lax.dot_general(
            gate_ref[rows, :], gate_w[cols, :], (((1,), (1,)), ((), ())), preferred_element_type=F32
        ) + lax.dot_general(up_ref[rows, :], up_w[cols, :], (((1,), (1,)), ((), ())), preferred_element_type=F32)

    def finish(rows, total):
        resid = resid_ref[rows, :]
        q = rsqrt_mean(resid)
        gain_out[...] += column_total(total * resid * q)
        weighed = gain_ref[...] * total
        pulled = q * weighed - resid * q * q * q * jnp.mean(weighed * resid, axis=-1, keepdims=True)
        return (cot_ref[rows, :].astype(F32) + pulled).astype(BF16)

    def weight_grad(source, target):
        def run(n, carry):
            cols = pl.ds(pl.multiple_of(n * step, step), step)
            target[cols, :] = lax.dot_general(
                two_ref[:, cols], source[...], (((0,), (0,)), ((), ())), preferred_element_type=F32
            ).astype(BF16)
            return carry

        def go():
            lax.fori_loop(0, features // step, run, 0)

        return go

    exchange(
        gate_ref.shape[0], features, product, finish,
        weight_grad(gate_ref, gate_grad), weight_grad(up_ref, up_grad), low_out, scratch,
    )


def pull(d_gate, d_up, gate_w, up_w, two_low, resid, cot, gain):
    tokens, hidden = d_gate.shape
    features = gate_w.shape[0]
    block = tokens // 4
    vmem = pl.BlockSpec(memory_space=pltpu.VMEM)
    return pl.pallas_call(
        pull_kernel,
        in_specs=[vmem] * 8,
        out_specs=[pl.BlockSpec(memory_space=pl.ANY), vmem, vmem, vmem],
        out_shape=[
            jax.ShapeDtypeStruct((tokens, features), BF16),
            jax.ShapeDtypeStruct((1, features), F32),
            jax.ShapeDtypeStruct((features, hidden), BF16),
            jax.ShapeDtypeStruct((features, hidden), BF16),
        ],
        scratch_shapes=exchange_scratch(block, features),
        compiler_params=params(46, collective_id=2, has_side_effects=True),
        cost_estimate=pl.CostEstimate(flops=8 * d_gate.size * features, bytes_accessed=tokens * features * 80, transcendentals=0),
        name="pull",
    )(d_gate, d_up, gate_w, up_w, two_low, resid, cot, gain)


def rsqrt_mean(v):
    return lax.rsqrt(jnp.mean(v * v, axis=-1, keepdims=True) + EPSILON)


def dot(a, b, left, right):
    return lax.dot_general(a, b, (((left,), (right,)), ((), ())), preferred_element_type=F32)


def body(
    n_dp,
    inputs,
    segment_ids,
    cotangent,
    first_gain,
    gate_weight,
    gate_bias,
    branch_weight,
    branch_bias,
    conv_weight,
    conv_bias,
    rate_weight,
    rate_bias,
    input_weight,
    input_bias,
    decay_param,
    out_weight,
    second_gain,
    ffn_gate,
    ffn_up,
    ffn_down,
):
    tokens, share = inputs.shape
    features = share * 4
    channels = gate_weight.shape[1]
    gain_one = first_gain.astype(F32)
    gain_two = second_gain.astype(F32)
    at = lax.axis_index("tensor")
    start = token_start(tokens)
    block = tokens // 4

    row = jnp.arange(tokens, dtype=jnp.int32)
    masks = []
    for k in range(4):
        offset = max(k, 1)
        earlier = jnp.concatenate([jnp.full((offset,), -1, jnp.int32), segment_ids[:-offset]])
        same = (row >= offset) & (segment_ids == earlier)
        masks.append(same if k else ~same)
    masks = jnp.pad(jnp.stack(masks, axis=1).astype(F32), ((0, HALO), (0, 0)))
    rows = jnp.concatenate(
        [
            conv_weight.astype(F32),
            jnp.concatenate([conv_bias, rate_bias, input_bias]).astype(F32).reshape(3, channels),
            jax.nn.softplus(-decay_param)[None],
        ]
    )

    across, masks, rows, gate_bias, branch_bias, gain_one, gain_two = lax.optimization_barrier(
        (swap_x(inputs), masks, rows, gate_bias.astype(F32), branch_bias.astype(F32), gain_one, gain_two)
    )
    in_pieces = (inputs, swap_core(inputs), across, swap_core(across))
    later_cot, _ = lax.optimization_barrier((cotangent, across))
    cot_across = swap_x(later_cot)
    whole_in = join_features(in_pieces)
    in_f = whole_in.astype(F32)
    q_one = rsqrt_mean(in_f)
    normed_low = lax.optimization_barrier((in_f * q_one * gain_one).astype(BF16))
    gate_pre = dot(normed_low, gate_weight, 1, 0) + gate_bias.astype(F32)
    branch_pre = dot(normed_low, branch_weight, 1, 0) + branch_bias.astype(F32)
    conv, rate, opened, state, mixed_low = forward_block(
        gate_pre, branch_pre, masks, rows, rate_weight, input_weight
    )
    mixed_low, cot_across = lax.optimization_barrier((mixed_low, cot_across))
    whole_cot = join_features((cotangent, swap_core(cotangent), cot_across, swap_core(cot_across)))
    two_low, resid = project(
        mixed_low, out_weight, lax.dynamic_slice_in_dim(whole_in, start, block, 0), gain_two[None]
    )
    d_hidden = dot(whole_cot, ffn_down, 1, 1)
    hidden_gate = dot(two_low, ffn_gate, 1, 0)
    hidden_up = dot(two_low, ffn_up, 1, 0)
    hidden_act, hidden_slope = gelu_parts(hidden_gate)
    hidden_low = (hidden_act * hidden_up).astype(BF16)
    cut = hidden_low.shape[1] * 5 // 9
    down_early = dot(hidden_low[:, :cut], whole_cot, 0, 0)
    down_late = dot(hidden_low[:, cut:], whole_cot, 0, 0)
    d_hgate = (d_hidden * hidden_up * hidden_slope).astype(BF16)
    d_hup = (d_hidden * hidden_act).astype(BF16)
    if n_dp == 8:
        down_early, down_late, d_hgate, d_hup = lax.optimization_barrier(
            (down_early.astype(BF16), down_late.astype(BF16), d_hgate, d_hup)
        )
        down_early = lax.psum(down_early, "dp")
    cot_mine = lax.dynamic_slice_in_dim(whole_cot, start, block, 0)
    d_resid_low, second_gain_grad, ffn_gate_grad, ffn_up_grad = pull(
        d_hgate, d_hup, ffn_gate, ffn_up, two_low, resid, cot_mine, gain_two[None]
    )
    second_gain_grad = second_gain_grad[0]
    d_mixed = dot(d_resid_low, out_weight, 1, 1)
    d_gate_low, d_branch_low, misc = backward_block(
        d_mixed, gate_pre, branch_pre, conv, rate, opened, state, masks, rows, rate_weight, input_weight
    )
    first_share = dot(d_gate_low, gate_weight, 1, 1) + dot(d_branch_low, branch_weight, 1, 1)
    product = first_share * in_f
    sums = jnp.concatenate([
        jnp.sum(product * q_one, axis=0), second_gain_grad, jnp.sum(product * gain_one, axis=1)
    ])
    sums = tensor_sum(sums.reshape(-1, LANES)).reshape(-1)
    if n_dp == 8:
        down_early, down_late, sums = lax.optimization_barrier((down_early, down_late, sums))
        down_late = lax.psum(down_late, "dp")
    gains = sums[: 2 * features].reshape(-1, channels)
    mean_one = sums[2 * features :, None] / features
    misc = lax.dynamic_update_slice_in_dim(misc, gains.astype(BF16), 2 * LANES + 16, 0)
    if n_dp == 8:
        (ffn_gate_grad, ffn_up_grad, misc, *summed), output, d_first = ring_all(
            [ffn_gate_grad, ffn_up_grad, misc],
            normed_low, d_gate_low, d_branch_low, mixed_low, d_resid_low, hidden_low, ffn_down, resid, first_share,
        )
        summed = [ffn_gate_grad, ffn_up_grad, *summed, misc]
        (*summed, down_late) = lax.optimization_barrier((*summed, down_late))
        summed = [a.astype(F32) for a in (jnp.concatenate([down_early, down_late]), *summed)]
    else:
        gate_weight_grad = dot(normed_low, d_gate_low, 0, 0)
        branch_weight_grad = dot(normed_low, d_branch_low, 0, 0)
        out_weight_grad = dot(mixed_low, d_resid_low, 0, 0)
        summed = [ffn_gate_grad, ffn_up_grad, gate_weight_grad, branch_weight_grad, out_weight_grad, misc]
        summed = dp_sum([jnp.concatenate([down_early, down_late]), *summed], n_dp)
        first_here, first_there = scatter_features(first_share)
        d_first = first_here + first_there.astype(F32)
        ffn_part = dot(hidden_low, ffn_down, 1, 0)
        with_resid = lax.dynamic_slice_in_dim(ffn_part, start, block, 0) + resid
        ffn_part = lax.dynamic_update_slice_in_dim(ffn_part, with_resid, start, 0)
        output_here, output_there = scatter_features(ffn_part)
        output = (output_here + output_there.astype(F32)).astype(BF16)
    ffn_down_grad, ffn_gate_grad, ffn_up_grad, gate_weight_grad, branch_weight_grad, out_weight_grad, misc = summed

    own_in = inputs.astype(F32)
    own_gain = lax.dynamic_slice_in_dim(gain_one, at * share, share, 0)
    input_grad = (
        lax.dynamic_slice_in_dim(d_resid_low, at * share, share, 1).astype(F32)
        + q_one * own_gain * d_first
        - own_in * q_one * q_one * q_one * mean_one
    )
    heads = rate_weight.shape[0]

    def blocks(v):
        return v.reshape(LANES, heads, LANES).transpose(1, 0, 2)

    small = misc[2 * LANES : 2 * LANES + 16]
    gains = misc[2 * LANES + 16 : 2 * LANES + 16 + gains.shape[0]].reshape(2, features)
    decay_grad = -small[7] * jax.nn.sigmoid(-decay_param)
    return (
        output,
        input_grad,
        gains[0],
        gate_weight_grad,
        small[8],
        branch_weight_grad,
        small[9],
        small[0:4],
        small[4],
        blocks(misc[:LANES]),
        small[5],
        blocks(misc[LANES : 2 * LANES]),
        small[6],
        decay_grad,
        out_weight_grad,
        gains[1],
        ffn_gate_grad,
        ffn_up_grad,
        ffn_down_grad,
    )


def solution(mesh):
    in_specs = (
        P("dp", "tensor"),
        P("dp"),
        P("dp", "tensor"),
        P(),
        P(None, "tensor"),
        P("tensor"),
        P(None, "tensor"),
        P("tensor"),
        P(None, "tensor"),
        P("tensor"),
        P("tensor", None, None),
        P("tensor"),
        P("tensor", None, None),
        P("tensor"),
        P("tensor"),
        P("tensor", None),
        P(),
        P(None, "tensor"),
        P(None, "tensor"),
        P("tensor", None),
    )
    out_specs = (
        P("dp", "tensor"),
        P("dp", "tensor"),
        P(),
        P(None, "tensor"),
        P("tensor"),
        P(None, "tensor"),
        P("tensor"),
        P(None, "tensor"),
        P("tensor"),
        P("tensor", None, None),
        P("tensor"),
        P("tensor", None, None),
        P("tensor"),
        P("tensor"),
        P("tensor", None),
        P(),
        P(None, "tensor"),
        P(None, "tensor"),
        P("tensor", None),
    )
    return jax.shard_map(
        functools.partial(body, mesh.shape["dp"]), mesh=mesh, in_specs=in_specs, out_specs=out_specs, check_vma=False
    )
```
